128 devices in a mesh: docs: 16 (over y, x_lo, core), vocab: 8 (over z, x_hi).
Axes of the slice: x: 4 (x_hi: 2, x_lo: 2; x = x_hi * 2 + x_lo), y: 4, z: 4, core: 2. Of those that a mesh axis runs over, the one named last changes fastest.
Arguments:
- doc_topics: bfloat16 [32768, 256], P('docs'), may hold values from 0.099609375 to 10
- word_topics: bfloat16 [65536, 256], P('vocab'), may hold values from 0.099609375 to 10
- word_weights: float32 [65536], P('vocab'), may hold values from 1 to 10
- tile_pairs: int32 [16, 8, 96], P('docs', 'vocab'), may hold values from 0 to 255, as said below
- tile_counts: bfloat16 [16, 8, 96, 512, 128], P('docs', 'vocab'), may hold values from 0 to 3
- tile_load: int32 [16, 8], P('docs', 'vocab'), may hold values from 1 to 96, as said below
Outputs:
- doc_next: float32 [32768, 256], P('docs')
- word_next: float32 [65536, 256], P(('vocab', 'docs'))
The draws below stay inside these ranges and needn't reach their ends.
Inputs may be any that keep to these rules, and one draw needn't show every extreme that they name: `tile_pairs`: A device's entries are distinct; entry p names document block p // 64 and word block p % 64 of the device's own documents and words. Only the first tile_load slots of a device's list hold its tiles; later slots hold entries and frequencies that are no tiles. Some device has exactly 96 tiles.
All inputs are finite; a program needn't handle non-finite values.
Results may differ from the reference program's by a relative error of at most 0.00095.
Values may be sent and summed in bfloat16 or wider, within the bound.
No kernel may reach another device: no remote copies, remote signals or barrier semaphores. Data moves between devices by JAX's collectives and lax.ppermute only.
A program may use at most 128 MiB of HBM per device.

```python
import math
import jax
import jax.numpy as jnp
from jax import lax

K = 256
V = 65536
TILE_DOCS = 512
TILE_WORDS = 128
DB_DEV = 4
NT_MAX = 96
WB_DEV = 64
DOCS = 32768
N_DOCS = 16
N_VOCAB = 8


def draw_tile_pairs(key, part):
    device_keys = jax.random.split(key, N_DOCS * N_VOCAB)

    def one_device(device_key):
        orders = jax.random.permutation(device_key, DB_DEV * WB_DEV)
        return orders[:NT_MAX].astype(jnp.int32)
    lists = jax.vmap(one_device)(device_keys)
    return lists.reshape(N_DOCS, N_VOCAB, NT_MAX).astype(jnp.int32)


def draw_tile_load(key, part):
    key_base = jax.random.fold_in(key, 11)
    key_heavy = jax.random.fold_in(key, 12)
    key_chosen = jax.random.fold_in(key, 13)
    key_busiest = jax.random.fold_in(key, 14)
    smallest = max(NT_MAX // 6, 1)
    typical = jax.random.randint(key_base, (N_DOCS * N_VOCAB,), smallest, NT_MAX // 2 + 1)
    heavier = jax.random.randint(key_heavy, (N_DOCS * N_VOCAB,), NT_MAX // 2, NT_MAX + 1)
    chosen = jax.random.randint(key_chosen, (N_DOCS * N_VOCAB,), 0, 8) == 0
    flattened = jnp.where(chosen, heavier, typical)
    busiest = jax.random.randint(key_busiest, (), 0, N_DOCS * N_VOCAB)
    flattened = jnp.where(jnp.arange(N_DOCS * N_VOCAB, dtype=jnp.int32) == busiest, NT_MAX, flattened)
    return flattened.reshape(N_DOCS, N_VOCAB).astype(jnp.int32)


def shard_levels(rng, extent, cuts, low, high):
    def one(position, shards_of):
        steps = jax.random.uniform(jax.random.fold_in(jax.random.fold_in(rng, 6), position), (shards_of,), jnp.float32, low / len(cuts), high / len(cuts))
        return jnp.repeat(jnp.exp(steps), extent[position] // shards_of).reshape((-1,) + (1,) * (len(extent) - position - 1))

    gain = one(*cuts[0])
    for cut in cuts[1:]:
        gain = gain * one(*cut)
    return gain


def setup_inputs(seed: int = 0) -> dict:
    key_of = jax.random.split(jax.random.key(seed), 7)
    return {
        "doc_topics": jnp.clip(jnp.exp(math.log(10.0) - 4.609084 * jax.random.uniform(key_of[0], (DOCS, K), jnp.float32) ** shard_levels(key_of[0], (DOCS, K), ((0, 16),), -0.2, 0.2)), 0.099609375, 10.0).astype(jnp.bfloat16),
        "word_topics": jnp.clip(jnp.exp(math.log(10.0) - 4.609084 * jax.random.uniform(key_of[1], (V, K), jnp.float32) ** shard_levels(key_of[1], (V, K), ((0, 8),), -0.2, 0.2)), 0.099609375, 10.0).astype(jnp.bfloat16),
        "word_weights": jnp.clip(jnp.exp(math.log(10.0) - 2.3025851 * jax.random.uniform(key_of[2], (V,), jnp.float32) ** shard_levels(key_of[2], (V,), ((0, 8),), -0.2, 0.2)), 1.0, 10.0),
        "tile_pairs": draw_tile_pairs(jax.random.fold_in(key_of[6], 71), 0),
        "tile_counts": jnp.clip(3.0 * jax.random.uniform(key_of[4], (N_DOCS, N_VOCAB, NT_MAX, TILE_DOCS, TILE_WORDS), jnp.float32) ** shard_levels(key_of[4], (N_DOCS, N_VOCAB, NT_MAX, TILE_DOCS, TILE_WORDS), ((0, 16), (1, 8)), -0.2, 0.2), 0.0, 3.0).astype(jnp.bfloat16),
        "tile_load": draw_tile_load(jax.random.fold_in(key_of[6], 71), 0),
    }


prior_doc = 0.5
prior_word = 0.01


def add_rows(total, start, addend):
    current = lax.dynamic_slice_in_dim(total, start, addend.shape[0], 0)
    return lax.dynamic_update_slice_in_dim(total, current + addend, start, 0)


def reference(doc_topics, word_topics, word_weights, tile_pairs, tile_counts, tile_load):
    doc_shards, word_shards, slot_count = tile_pairs.shape
    tile_docs = tile_counts.shape[3]
    tile_words = tile_counts.shape[4]
    doc_rows = doc_topics.shape[0] // doc_shards
    word_rows = word_topics.shape[0] // word_shards
    blocks = word_rows // tile_words
    topics = doc_topics.shape[1]
    flat_ids = jnp.arange(doc_shards * word_shards * slot_count, dtype=jnp.int32)
    doc_shard = flat_ids // (word_shards * slot_count)
    word_shard = (flat_ids // slot_count) % word_shards
    tile_slot = flat_ids % slot_count
    tile_loads = tile_load.reshape(-1)[flat_ids // slot_count]
    is_live = tile_slot < tile_loads
    pair_list = tile_pairs.reshape(-1).astype(jnp.int32)
    doc_start = (doc_shard * doc_rows + (pair_list // blocks) * tile_docs).astype(jnp.int32)
    word_start = (word_shard * word_rows + (pair_list % blocks) * tile_words).astype(jnp.int32)
    counts_flat = tile_counts.reshape(-1, tile_docs, tile_words)

    def tile_step(running, tile_entry):
        doc_part, word_part = running
        live_flag, start_doc, start_word, frequencies = tile_entry

        def tile_work(unused):
            doc_rows_here = lax.dynamic_slice_in_dim(doc_topics, start_doc, tile_docs, 0)
            word_rows_here = lax.dynamic_slice_in_dim(word_topics, start_word, tile_words, 0)
            weight_rows = lax.dynamic_slice_in_dim(word_weights, start_word, tile_words, 0)
            weighted = (frequencies.astype(jnp.float32) * weight_rows[None, :]).astype(jnp.bfloat16)
            predicted = jnp.dot(doc_rows_here, word_rows_here.T, preferred_element_type=jnp.float32)
            count_ratio = (weighted.astype(jnp.float32) / predicted).astype(jnp.bfloat16)
            doc_terms = jnp.dot(count_ratio, word_rows_here, preferred_element_type=jnp.float32)
            word_terms = jnp.dot(count_ratio.T, doc_rows_here, preferred_element_type=jnp.float32)
            return doc_terms, word_terms

        def skipped(unused):
            return (jnp.zeros((tile_docs, topics), jnp.float32), jnp.zeros((tile_words, topics), jnp.float32))

        doc_terms, word_terms = lax.cond(live_flag, tile_work, skipped, 0)
        return (add_rows(doc_part, start_doc, doc_terms), add_rows(word_part, start_word, word_terms)), None

    initial = (jnp.zeros(doc_topics.shape, jnp.float32), jnp.zeros(word_topics.shape, jnp.float32))
    (doc_sums, word_sums), unused = lax.scan(tile_step, initial, (is_live, doc_start, word_start, counts_flat))
    doc_scaled = doc_topics.astype(jnp.float32) * doc_sums + prior_doc
    doc_next = topics * doc_scaled / jnp.sum(doc_scaled, axis=1, keepdims=True)
    word_scaled = word_topics.astype(jnp.float32) * word_sums + prior_word
    word_next = word_topics.shape[0] * word_scaled / jnp.sum(word_scaled, axis=0, keepdims=True)
    return doc_next, word_next
```

```python
import functools

import jax
import jax.numpy as jnp
from jax import lax
from jax.experimental import pallas as pl
from jax.experimental.pallas import tpu as pltpu
from jax.sharding import PartitionSpec as P

prior_doc = 0.5
prior_word = 0.01
SLOTS = 4


def tiles_kernel(
    pairs_ref,
    load_ref,
    doc_hbm,
    word_hbm,
    weights_ref,
    counts_hbm,
    doc_out,
    word_out,
    doc_rows,
    word_rows,
    counts_buf,
    first_slot,
    second_slot,
    item_doc,
    pending,
    topics_sem,
    counts_sem,
):
    tile_docs, tile_words = counts_hbm.shape[1:]
    blocks = word_hbm.shape[0] // tile_words
    doc_blocks = doc_hbm.shape[0] // tile_docs
    load = load_ref[0]

    doc_copy = pltpu.make_async_copy(doc_hbm, doc_rows, topics_sem.at[0])
    word_copy = pltpu.make_async_copy(word_hbm, word_rows, topics_sem.at[1])
    doc_copy.start()
    word_copy.start()

    for b in range(doc_blocks):
        pending[b] = -1

    def sort_slot(s, made):
        b = pairs_ref[s] // blocks
        waiting = pending[b]
        first_slot[made] = waiting
        second_slot[made] = s
        item_doc[made] = b
        pending[b] = jnp.where(waiting >= 0, -1, s)
        return made + jnp.where(waiting >= 0, 1, 0)

    made = lax.fori_loop(0, load, sort_slot, 0)
    for b in range(doc_blocks):
        waiting = pending[b]
        first_slot[made] = waiting
        second_slot[made] = -1
        item_doc[made] = b
        made = made + jnp.where(waiting >= 0, 1, 0)

    def copies(item):
        ring = lax.rem(item, SLOTS)
        first = first_slot[item]
        second = second_slot[item]
        second = jnp.where(second >= 0, second, first)
        return (
            pltpu.make_async_copy(
                counts_hbm.at[first], counts_buf.at[ring, 0], counts_sem.at[ring, 0]
            ),
            pltpu.make_async_copy(
                counts_hbm.at[second], counts_buf.at[ring, 1], counts_sem.at[ring, 1]
            ),
        )

    def start(item):
        for copy in copies(item):
            copy.start()

    for ahead in range(SLOTS - 1):

        @pl.when(ahead < made)
        def _():
            start(ahead)

    doc_out[...] = jnp.zeros_like(doc_out)
    word_out[...] = jnp.zeros_like(word_out)
    doc_copy.wait()
    word_copy.wait()

    def run_item(item, carry):
        @pl.when(item + SLOTS - 1 < made)
        def _():
            start(item + SLOTS - 1)

        ring = lax.rem(item, SLOTS)
        first = first_slot[item]
        second = second_slot[item]
        paired = second >= 0
        first_block = lax.rem(pairs_ref[first], blocks)
        second_block = lax.rem(pairs_ref[jnp.where(paired, second, first)], blocks)
        doc_at = pl.ds(pl.multiple_of(item_doc[item] * tile_docs, tile_docs), tile_docs)
        first_at = pl.ds(pl.multiple_of(first_block * tile_words, tile_words), tile_words)
        second_at = pl.ds(pl.multiple_of(second_block * tile_words, tile_words), tile_words)
        words = jnp.concatenate([word_rows[first_at, :], word_rows[second_at, :]], axis=0)
        docs = doc_rows[doc_at, :]
        weight = jnp.concatenate(
            [
                weights_ref[pl.ds(first_block, 1), :],
                weights_ref[pl.ds(second_block, 1), :] * jnp.where(paired, 1.0, 0.0),
            ],
            axis=1,
        )
        for copy in copies(item):
            copy.wait()
        predicted = lax.dot_general(
            docs, words, (((1,), (1,)), ((), ())), preferred_element_type=jnp.float32
        )
        counts = jnp.concatenate([counts_buf[ring, 0], counts_buf[ring, 1]], axis=1)
        weighted = (counts.astype(jnp.float32) * weight).astype(jnp.bfloat16)
        ratio = (weighted.astype(jnp.float32) / predicted).astype(jnp.bfloat16)
        doc_out[doc_at, :] += jnp.dot(ratio, words, preferred_element_type=jnp.float32)
        terms = lax.dot_general(
            ratio, docs, (((0,), (0,)), ((), ())), preferred_element_type=jnp.float32
        )
        word_out[first_at, :] += terms[:tile_words]
        word_out[second_at, :] += terms[tile_words:]
        return carry

    lax.fori_loop(0, made, run_item, 0)


def run_tiles(pair_list, own_load, doc_topics, word_topics, weight_table, counts_all):
    slots = pair_list.shape[0]
    tile_docs, tile_words = counts_all.shape[1:]
    doc_blocks = doc_topics.shape[0] // tile_docs
    items = slots + doc_blocks + 8
    return pl.pallas_call(
        tiles_kernel,
        out_shape=(
            jax.ShapeDtypeStruct(doc_topics.shape, jnp.float32),
            jax.ShapeDtypeStruct(word_topics.shape, jnp.float32),
        ),
        in_specs=[
            pl.BlockSpec(memory_space=pltpu.SMEM),
            pl.BlockSpec(memory_space=pltpu.SMEM),
            pl.BlockSpec(memory_space=pl.ANY),
            pl.BlockSpec(memory_space=pl.ANY),
            pl.BlockSpec(memory_space=pltpu.VMEM),
            pl.BlockSpec(memory_space=pl.ANY),
        ],
        out_specs=(
            pl.BlockSpec(memory_space=pltpu.VMEM),
            pl.BlockSpec(memory_space=pltpu.VMEM),
        ),
        scratch_shapes=[
            pltpu.VMEM(doc_topics.shape, doc_topics.dtype),
            pltpu.VMEM(word_topics.shape, word_topics.dtype),
            pltpu.VMEM((SLOTS, 2, tile_docs, tile_words), counts_all.dtype),
            pltpu.SMEM((items,), jnp.int32),
            pltpu.SMEM((items,), jnp.int32),
            pltpu.SMEM((items,), jnp.int32),
            pltpu.SMEM((doc_blocks,), jnp.int32),
            pltpu.SemaphoreType.DMA((2,)),
            pltpu.SemaphoreType.DMA((SLOTS, 2)),
        ],
        compiler_params=pltpu.CompilerParams(vmem_limit_bytes=48 << 20),
        name="tiles",
    )(pair_list, own_load, doc_topics, word_topics, weight_table, counts_all)


def on_device(doc_topics, word_topics, word_weights, tile_pairs, tile_counts, tile_load):
    counts_all = tile_counts[0, 0]
    tile_words = counts_all.shape[2]
    blocks = word_topics.shape[0] // tile_words
    weight_table = word_weights.reshape(blocks, tile_words)
    doc_part, word_part = run_tiles(
        tile_pairs[0, 0], tile_load[0], doc_topics, word_topics, weight_table, counts_all
    )
    doc_sums = lax.psum(doc_part, "vocab")
    doc_scaled = doc_topics.astype(jnp.float32) * doc_sums + prior_doc
    doc_next = doc_topics.shape[1] * doc_scaled / jnp.sum(doc_scaled, axis=1, keepdims=True)
    row_count = word_topics.shape[0] // lax.axis_size("docs")
    docs_index = lax.axis_index("docs")
    word_sums = lax.psum_scatter(word_part, "docs", scatter_dimension=0, tiled=True)
    own_words = lax.dynamic_slice_in_dim(word_topics, docs_index * row_count, row_count, 0)
    word_scaled = own_words.astype(jnp.float32) * word_sums + prior_word
    column = lax.psum(jnp.sum(word_scaled, axis=0), ("docs", "vocab"))
    vocab_total = word_topics.shape[0] * lax.axis_size("vocab")
    word_next = vocab_total * word_scaled / column[None, :]
    return (doc_next, word_next)


def solution(mesh):
    placed = (
        P("docs", None),
        P("vocab", None),
        P("vocab"),
        P("docs", "vocab", None),
        P("docs", "vocab", None, None, None),
        P("docs", "vocab"),
    )
    return jax.shard_map(
        on_device,
        mesh=mesh,
        in_specs=placed,
        out_specs=(P("docs", None), P(("vocab", "docs"), None)),
        check_vma=False,
    )
```

```python
import jax
import jax.numpy as jnp
from jax import lax
from jax.experimental import pallas as pl
from jax.experimental.pallas import tpu as pltpu
from jax.sharding import PartitionSpec as P

prior_doc = 0.5
prior_word = 0.01
SLOTS = 4
N_Y, N_X_LO, N_CORE = 4, 2, 2
N_Z, N_X_HI = 4, 2
WORD_SCALE = 2.0**-7
DOC_SCALE = 2.0**-8


def tiles_kernel(
    pairs_ref,
    load_ref,
    docs_index_ref,
    vocab_index_ref,
    doc_hbm,
    word_hbm,
    weights_ref,
    counts_hbm,
    doc_parts_out,
    keep_out,
    send_out,
    column_out,
    doc_sums,
    word_sums,
    doc_rows,
    word_rows,
    counts_buf,
    first_slot,
    second_slot,
    item_doc,
    pending,
    topics_sem,
    counts_sem,
    sums_sem,
):
    tile_docs, tile_words = counts_hbm.shape[1:]
    blocks = word_hbm.shape[0] // tile_words
    doc_blocks = doc_hbm.shape[0] // tile_docs
    load = load_ref[0]
    y, own_core = docs_index_ref[0] // (N_X_LO * N_CORE), lax.rem(docs_index_ref[0], N_CORE)
    z = vocab_index_ref[0] // N_X_HI
    dest_blocks = blocks // (N_Y * N_X_LO * N_CORE)

    def word_place(block):
        dest = block // dest_blocks
        core = lax.rem(dest, N_CORE)
        x_lo = lax.rem(dest // N_CORE, N_X_LO)
        step = lax.rem(dest // (N_CORE * N_X_LO) - y + N_Y, N_Y)
        other = jnp.where(core == own_core, 0, 1)
        return ((other * N_Y + step) * N_X_LO + x_lo) * dest_blocks + lax.rem(block, dest_blocks)

    doc_copy = pltpu.make_async_copy(doc_hbm, doc_rows, topics_sem.at[0])
    word_copy = pltpu.make_async_copy(word_hbm, word_rows, topics_sem.at[1])
    doc_copy.start()
    word_copy.start()

    for b in range(doc_blocks):
        pending[b] = -1

    def sort_slot(s, made):
        b = pairs_ref[s] // blocks
        waiting = pending[b]
        first_slot[made] = waiting
        second_slot[made] = s
        item_doc[made] = b
        pending[b] = jnp.where(waiting >= 0, -1, s)
        return made + jnp.where(waiting >= 0, 1, 0)

    made = lax.fori_loop(0, load, sort_slot, 0)
    for b in range(doc_blocks):
        waiting = pending[b]
        first_slot[made] = waiting
        second_slot[made] = -1
        item_doc[made] = b
        made = made + jnp.where(waiting >= 0, 1, 0)

    def copies(item):
        ring = lax.rem(item, SLOTS)
        first = first_slot[item]
        second = second_slot[item]
        second = jnp.where(second >= 0, second, first)
        return (
            pltpu.make_async_copy(
                counts_hbm.at[first], counts_buf.at[ring, 0], counts_sem.at[ring, 0]
            ),
            pltpu.make_async_copy(
                counts_hbm.at[second], counts_buf.at[ring, 1], counts_sem.at[ring, 1]
            ),
        )

    def start(item):
        for copy in copies(item):
            copy.start()

    for ahead in range(SLOTS - 1):

        @pl.when(ahead < made)
        def _():
            start(ahead)

    doc_sums[...] = jnp.zeros_like(doc_sums)
    word_sums[...] = jnp.zeros_like(word_sums)
    doc_copy.wait()
    word_copy.wait()

    def run_item(item, carry):
        @pl.when(item + SLOTS - 1 < made)
        def _():
            start(item + SLOTS - 1)

        ring = lax.rem(item, SLOTS)
        first = first_slot[item]
        second = second_slot[item]
        paired = second >= 0
        first_block = lax.rem(pairs_ref[first], blocks)
        second_block = lax.rem(pairs_ref[jnp.where(paired, second, first)], blocks)
        doc_at = pl.ds(pl.multiple_of(item_doc[item] * tile_docs, tile_docs), tile_docs)
        first_at = pl.ds(pl.multiple_of(first_block * tile_words, tile_words), tile_words)
        second_at = pl.ds(pl.multiple_of(second_block * tile_words, tile_words), tile_words)
        words = jnp.concatenate([word_rows[first_at, :], word_rows[second_at, :]], axis=0)
        docs = doc_rows[doc_at, :]
        weight = jnp.concatenate(
            [
                weights_ref[pl.ds(first_block, 1), :],
                weights_ref[pl.ds(second_block, 1), :] * jnp.where(paired, 1.0, 0.0),
            ],
            axis=1,
        )
        for copy in copies(item):
            copy.wait()
        predicted = lax.dot_general(
            docs, words, (((1,), (1,)), ((), ())), preferred_element_type=jnp.float32
        )
        counts = jnp.concatenate([counts_buf[ring, 0], counts_buf[ring, 1]], axis=1)
        weighted = (counts.astype(jnp.float32) * weight).astype(jnp.bfloat16)
        ratio = (weighted.astype(jnp.float32) / predicted).astype(jnp.bfloat16)
        doc_step = lax.rem(item_doc[item] - z + N_Z, N_Z)
        doc_to = pl.ds(pl.multiple_of(doc_step * tile_docs, tile_docs), tile_docs)
        doc_sums[doc_to, :] += jnp.dot(ratio, words, preferred_element_type=jnp.float32)
        terms = lax.dot_general(
            ratio, docs, (((0,), (0,)), ((), ())), preferred_element_type=jnp.float32
        )
        for block, part in ((first_block, terms[:tile_words]), (second_block, terms[tile_words:])):
            to = pl.multiple_of(word_place(block) * tile_words, tile_words)
            word_sums[pl.ds(to, tile_words), :] += part
        return carry

    lax.fori_loop(0, made, run_item, 0)

    outgoing = []
    rows = word_sums.shape[0] // (N_CORE * N_Y)
    for n, out in enumerate((keep_out, send_out)):
        for step in range(N_Y):
            outgoing.append((word_sums.at[pl.ds((n * N_Y + step) * rows, rows)], out[step]))
    for step in range(N_Z):
        outgoing.append((doc_sums.at[pl.ds(step * tile_docs, tile_docs)], doc_parts_out[step]))
    outgoing = [
        pltpu.make_async_copy(source, target, sums_sem.at[n])
        for n, (source, target) in enumerate(outgoing)
    ]
    for copy in outgoing:
        copy.start()
    column = jnp.zeros((1, doc_rows.shape[1]), jnp.float32)
    for step in range(N_Z):
        at = pl.multiple_of(lax.rem(z + step, N_Z) * tile_docs, tile_docs)
        topics = doc_rows[pl.ds(at, tile_docs), :].astype(jnp.float32)
        sums = doc_sums[pl.ds(step * tile_docs, tile_docs), :]
        column = column + jnp.sum(topics * sums, axis=0, keepdims=True)
    column_out[...] = column
    for copy in outgoing:
        copy.wait()


def run_tiles(
    pair_list, own_load, docs_index, vocab_index, doc_topics, word_topics, weight_table, counts_all
):
    slots = pair_list.shape[0]
    tile_docs, tile_words = counts_all.shape[1:]
    topics = doc_topics.shape[1]
    doc_blocks = doc_topics.shape[0] // tile_docs
    items = slots + doc_blocks + 8
    doc_part = jax.ShapeDtypeStruct((doc_topics.shape[0] // N_Z, topics), jnp.float32)
    word_part = jax.ShapeDtypeStruct((word_topics.shape[0] // (N_CORE * N_Y), topics), jnp.float32)
    smem = pl.BlockSpec(memory_space=pltpu.SMEM)
    hbm = pl.BlockSpec(memory_space=pl.ANY)
    return pl.pallas_call(
        tiles_kernel,
        out_shape=(
            (doc_part,) * N_Z,
            (word_part,) * N_Y,
            (word_part,) * N_Y,
            jax.ShapeDtypeStruct((1, topics), jnp.float32),
        ),
        in_specs=[smem] * 4 + [hbm, hbm, pl.BlockSpec(memory_space=pltpu.VMEM), hbm],
        out_specs=(
            (hbm,) * N_Z,
            (hbm,) * N_Y,
            (hbm,) * N_Y,
            pl.BlockSpec(memory_space=pltpu.VMEM),
        ),
        scratch_shapes=[
            pltpu.VMEM(doc_topics.shape, jnp.float32),
            pltpu.VMEM(word_topics.shape, jnp.float32),
            pltpu.VMEM(doc_topics.shape, doc_topics.dtype),
            pltpu.VMEM(word_topics.shape, word_topics.dtype),
            pltpu.VMEM((SLOTS, 2, tile_docs, tile_words), counts_all.dtype),
            pltpu.SMEM((items,), jnp.int32),
            pltpu.SMEM((items,), jnp.int32),
            pltpu.SMEM((items,), jnp.int32),
            pltpu.SMEM((doc_blocks,), jnp.int32),
            pltpu.SemaphoreType.DMA((2,)),
            pltpu.SemaphoreType.DMA((SLOTS, 2)),
            pltpu.SemaphoreType.DMA((N_Z + 2 * N_Y,)),
        ],
        compiler_params=pltpu.CompilerParams(vmem_limit_bytes=48 << 20),
        name="tiles",
    )(
        pair_list,
        own_load,
        docs_index,
        vocab_index,
        doc_topics,
        word_topics,
        weight_table,
        counts_all,
    )


def moves(axis, size, move):
    return lambda value: lax.ppermute(value, axis, [(n, move(n) % size) for n in range(size)])


def to_half(value):
    return value.astype(jnp.float16)


def to_float(value):
    return value.astype(jnp.float32)


def on_device(doc_topics, word_topics, word_weights, tile_pairs, tile_counts, tile_load):
    n_docs, n_vocab = lax.axis_size("docs"), lax.axis_size("vocab")
    docs_index, vocab_index = lax.axis_index("docs"), lax.axis_index("vocab")
    x_lo = docs_index // N_CORE % N_X_LO
    z, x_hi = vocab_index // N_X_HI, vocab_index % N_X_HI
    to_core = moves("docs", n_docs, lambda n: n ^ 1)
    to_x_lo = moves("docs", n_docs, lambda n: n ^ N_CORE)
    y_up = moves("docs", n_docs, lambda n: n + N_X_LO * N_CORE)
    y_down = moves("docs", n_docs, lambda n: n - N_X_LO * N_CORE)
    to_x_hi = moves("vocab", n_vocab, lambda n: n ^ 1)
    z_up = moves("vocab", n_vocab, lambda n: n + N_X_HI)
    z_down = moves("vocab", n_vocab, lambda n: n - N_X_HI)

    counts_all = tile_counts[0, 0]
    tile_words = counts_all.shape[2]
    blocks = word_topics.shape[0] // tile_words
    weight_table = word_weights.reshape(blocks, tile_words)
    doc_parts, keep, send, column = run_tiles(
        tile_pairs[0, 0],
        tile_load[0],
        docs_index.reshape(1),
        vocab_index.reshape(1),
        doc_topics,
        word_topics,
        weight_table,
        counts_all,
    )

    y_across = moves("docs", n_docs, lambda n: n + 2 * N_X_LO * N_CORE)
    z_across = moves("vocab", n_vocab, lambda n: n + 2 * N_X_HI)
    meet = lambda *values: lax.optimization_barrier(values)
    word_rows = keep[0].shape[0] // N_X_LO
    doc_rows = doc_parts[0].shape[0] // N_X_HI

    part = [piece * DOC_SCALE for piece in doc_parts]
    word_far = to_core(send[2])
    doc_up = z_up(to_half(part[2][:doc_rows]))
    doc_down = z_down(to_half(part[2][doc_rows:]))
    column = column + to_core(column)
    word_far, doc_up, doc_down, column = meet(word_far, doc_up, doc_down, column)

    far = (keep[2] + word_far) * WORD_SCALE
    word_up = y_up(to_half(far[:word_rows]))
    word_down = y_down(to_half(far[word_rows:]))
    from_core = {step: to_core(send[step]) for step in (1, 3, 0)}
    doc_below = z_up(
        to_half(jnp.concatenate([part[1][:doc_rows] + to_float(doc_up), part[1][doc_rows:]]))
    )
    doc_above = z_down(
        to_half(jnp.concatenate([part[3][:doc_rows], part[3][doc_rows:] + to_float(doc_down)]))
    )
    column = column + to_x_lo(column)
    column = column + to_x_hi(column)
    word_up, word_down, from_core[1], from_core[3], from_core[0], doc_below, doc_above, column = meet(
        word_up, word_down, from_core[1], from_core[3], from_core[0], doc_below, doc_above, column
    )

    near = {step: (keep[step] + from_core[step]) * WORD_SCALE for step in (1, 3, 0)}
    word_below = y_up(
        to_half(jnp.concatenate([near[1][:word_rows] + to_float(word_up), near[1][word_rows:]]))
    )
    word_above = y_down(
        to_half(jnp.concatenate([near[3][:word_rows], near[3][word_rows:] + to_float(word_down)]))
    )
    doc_pair = part[0] + to_float(doc_below) + to_float(doc_above)
    doc_mine = lax.dynamic_slice_in_dim(doc_pair, x_hi * doc_rows, doc_rows, 0)
    doc_other = lax.dynamic_slice_in_dim(doc_pair, (1 - x_hi) * doc_rows, doc_rows, 0)
    doc_sums = (doc_mine + to_float(to_x_hi(to_half(doc_other)))) / DOC_SCALE
    own_docs = lax.dynamic_slice_in_dim(doc_topics, vocab_index * doc_rows, doc_rows, 0)
    doc_scaled = own_docs.astype(jnp.float32) * doc_sums + prior_doc
    doc_block = to_half(
        doc_topics.shape[1] * doc_scaled / jnp.sum(doc_scaled, axis=1, keepdims=True)
    )
    doc_far = to_x_hi(doc_block)
    column = column + y_up(column)
    column = column + y_across(column)
    word_below, word_above, doc_block, doc_far, column = meet(
        word_below, word_above, doc_block, doc_far, column
    )

    word_pair = near[0] + to_float(word_below) + to_float(word_above)
    word_mine = lax.dynamic_slice_in_dim(word_pair, x_lo * word_rows, word_rows, 0)
    word_other = lax.dynamic_slice_in_dim(word_pair, (1 - x_lo) * word_rows, word_rows, 0)
    word_far = to_x_lo(to_half(word_other))
    doc_here = jnp.concatenate(
        [
            jnp.where(x_hi == 0, doc_block, doc_far),
            jnp.where(x_hi == 0, doc_far, doc_block),
        ]
    )
    doc_below, doc_above = z_up(doc_here), z_down(doc_here)
    column = column + z_up(column)
    column = column + z_across(column)
    word_far, doc_below, doc_above, column = meet(word_far, doc_below, doc_above, column)

    low_across, high_across = z_up(doc_below[:doc_rows]), z_down(doc_above[doc_rows:])
    word_sums = (word_mine + to_float(word_far)) / WORD_SCALE
    vocab_total = word_topics.shape[0] * n_vocab
    row_count = word_topics.shape[0] // n_docs
    own_words = lax.dynamic_slice_in_dim(word_topics, docs_index * row_count, row_count, 0)
    word_scaled = own_words.astype(jnp.float32) * word_sums + prior_word
    word_next = vocab_total * word_scaled / (column + vocab_total * prior_word)
    by_step = (doc_here, doc_above, jnp.concatenate([low_across, high_across]), doc_below)
    doc_next = jnp.concatenate(
        [to_float(lax.select_n((place - z) % N_Z, *by_step)) for place in range(N_Z)]
    )
    return (doc_next, word_next)


def solution(mesh):
    placed = (
        P("docs", None),
        P("vocab", None),
        P("vocab"),
        P("docs", "vocab", None),
        P("docs", "vocab", None, None, None),
        P("docs", "vocab"),
    )
    return jax.shard_map(
        on_device,
        mesh=mesh,
        in_specs=placed,
        out_specs=(P("docs", None), P(("vocab", "docs"), None)),
        check_vma=False,
    )
```

```python
import jax
import jax.numpy as jnp
from jax import lax
from jax.experimental import pallas as pl
from jax.experimental.pallas import tpu as pltpu
from jax.sharding import PartitionSpec as P

prior_doc = 0.5
prior_word = 0.01
SLOTS = 16
AT_ONCE = 4
N_Y, N_X_LO, N_CORE = 4, 2, 2
N_Z, N_X_HI = 4, 2
WORD_SCALE = 2.0**-7
DOC_SCALE = 2.0**-8
TOTAL_SCALE = 2.0**-9
TOTAL_ROWS = 16


def tiles_kernel(
    pairs_hbm,
    load_ref,
    docs_index_ref,
    vocab_index_ref,
    doc_hbm,
    word_hbm,
    weights_hbm,
    counts_hbm,
    doc_parts_out,
    keep_out,
    send_out,
    pairs_ref,
    weights_ref,
    doc_sums,
    word_sums,
    doc_rows,
    word_rows,
    counts_buf,
    first_slot,
    second_slot,
    item_doc,
    pending,
    topics_sem,
    counts_sem,
    sums_sem,
):
    tile_docs, tile_words = counts_hbm.shape[1:]
    blocks = word_hbm.shape[0] // tile_words
    doc_blocks = doc_hbm.shape[0] // tile_docs
    load = load_ref[0, 0]
    y, own_core = docs_index_ref[0] // (N_X_LO * N_CORE), lax.rem(docs_index_ref[0], N_CORE)
    z = vocab_index_ref[0] // N_X_HI
    dest_blocks = blocks // (N_Y * N_X_LO * N_CORE)

    part_rows = dest_blocks * tile_words + TOTAL_ROWS

    def word_place(block):
        dest = block // dest_blocks
        core = lax.rem(dest, N_CORE)
        x_lo = lax.rem(dest // N_CORE, N_X_LO)
        step = lax.rem(dest // (N_CORE * N_X_LO) - y + N_Y, N_Y)
        other = jnp.where(core == own_core, 0, 1)
        place = jnp.where(step == 0, 3, jnp.where(step == 2, 0, (step + 1) // 2))
        return ((other * N_Y + place) * N_X_LO + x_lo) * part_rows + (
            lax.rem(block, dest_blocks) * tile_words
        )

    doc_copy = pltpu.make_async_copy(doc_hbm, doc_rows, topics_sem.at[0])
    word_copy = pltpu.make_async_copy(word_hbm, word_rows, topics_sem.at[1])
    pairs_copy = pltpu.make_async_copy(pairs_hbm.at[0], pairs_ref, topics_sem.at[2])
    weights_copy = pltpu.make_async_copy(weights_hbm, weights_ref, topics_sem.at[3])
    pairs_copy.start()
    doc_copy.start()
    word_copy.start()
    weights_copy.start()

    for b in range(doc_blocks):
        pending[b] = -1

    pairs_copy.wait()

    def sort_slot(s, made):
        b = pairs_ref[0, s] // blocks
        waiting = pending[b]
        first_slot[made] = waiting
        second_slot[made] = s
        item_doc[made] = b
        pending[b] = jnp.where(waiting >= 0, -1, s)
        return made + jnp.where(waiting >= 0, 1, 0)

    made = lax.fori_loop(0, load, sort_slot, 0)
    for b in range(doc_blocks):
        waiting = pending[b]
        first_slot[made] = waiting
        second_slot[made] = -1
        item_doc[made] = b
        made = made + jnp.where(waiting >= 0, 1, 0)

    def pad_item(n, carry):
        first_slot[made + n] = -1
        second_slot[made + n] = -1
        item_doc[made + n] = 0
        return carry

    lax.fori_loop(0, AT_ONCE - 1, pad_item, 0)
    rounds = (made + AT_ONCE - 1) // AT_ONCE

    def copies(item):
        ring = lax.rem(item, SLOTS)
        return [
            pltpu.make_async_copy(
                counts_hbm.at[jnp.maximum(slots[item], 0)],
                counts_buf.at[ring, n],
                counts_sem.at[ring, n],
            )
            for n, slots in enumerate((first_slot, second_slot))
        ]

    def start(n):
        @pl.when(n < rounds)
        def _():
            for item in range(AT_ONCE):
                for copy in copies(n * AT_ONCE + item):
                    copy.start()

    for ahead in range(SLOTS // AT_ONCE - 1):
        start(ahead)

    doc_sums[...] = jnp.zeros_like(doc_sums)
    word_sums[...] = jnp.zeros_like(word_sums)
    doc_copy.wait()
    word_copy.wait()
    weights_copy.wait()

    def load_item(item):
        doc_at = pl.multiple_of(item_doc[item] * tile_docs, tile_docs)
        docs = doc_rows[pl.ds(doc_at, tile_docs), :]
        words, weight, counts, word_blocks = [], [], [], []
        for n, slots in enumerate((first_slot, second_slot)):
            block = lax.rem(pairs_ref[0, jnp.maximum(slots[item], 0)], blocks)
            word_at = pl.multiple_of(block * tile_words, tile_words)
            words.append(word_rows[pl.ds(word_at, tile_words), :])
            live = jnp.where(slots[item] >= 0, 1.0, 0.0)
            weight.append(weights_ref[pl.ds(block, 1), :] * live)
            counts.append(counts_buf[lax.rem(item, SLOTS), n])
            word_blocks.append(block)
        words = jnp.concatenate(words, axis=0)
        weight = jnp.concatenate(weight, axis=1)
        counts = jnp.concatenate(counts, axis=1)
        return docs, words, weight, counts, word_blocks

    def count_ratio(docs, words, weight, counts):
        predicted = lax.dot_general(
            docs, words, (((1,), (1,)), ((), ())), preferred_element_type=jnp.float32
        )
        weighted = (counts.astype(jnp.float32) * weight).astype(jnp.bfloat16)
        return (weighted.astype(jnp.float32) / predicted).astype(jnp.bfloat16)

    def add_terms(item, ratio, docs, words, word_blocks):
        doc_step = lax.rem(item_doc[item] - z + N_Z, N_Z)
        doc_to = pl.ds(pl.multiple_of(doc_step * tile_docs, tile_docs), tile_docs)
        doc_sums[doc_to, :] += jnp.dot(ratio, words, preferred_element_type=jnp.float32)
        terms = lax.dot_general(
            ratio, docs, (((0,), (0,)), ((), ())), preferred_element_type=jnp.float32
        )
        for n, block in enumerate(word_blocks):
            to = pl.multiple_of(word_place(block), TOTAL_ROWS)
            word_sums[pl.ds(to, tile_words), :] += terms[n * tile_words : (n + 1) * tile_words]

    def run_items(n, carry):
        start(n + SLOTS // AT_ONCE - 1)
        items = [n * AT_ONCE + item for item in range(AT_ONCE)]
        for item in items:
            for copy in copies(item):
                copy.wait()
        loaded = [load_item(item) for item in items]
        ratios = [count_ratio(*fields[:4]) for fields in loaded]
        for item, ratio, (docs, words, _, _, word_blocks) in zip(items, ratios, loaded):
            add_terms(item, ratio, docs, words, word_blocks)
        return carry

    lax.fori_loop(0, rounds, run_items, 0)

    def leave(n, source, target):
        copy = pltpu.make_async_copy(source, target, sums_sem.at[n])
        copy.start()
        return copy

    leaving = [
        leave(step, doc_sums.at[pl.ds(step * tile_docs, tile_docs)], doc_parts_out[step])
        for step in range(N_Z)
    ]
    total = jnp.zeros((1, doc_rows.shape[1]), jnp.float32)
    for step in range(N_Z):
        at = pl.multiple_of(lax.rem(z + step, N_Z) * tile_docs, tile_docs)
        topics = doc_rows[pl.ds(at, tile_docs), :].astype(jnp.float32)
        sums = doc_sums[pl.ds(step * tile_docs, tile_docs), :]
        total = total + jnp.sum(topics * sums, axis=0, keepdims=True)
    total = jnp.broadcast_to(total * TOTAL_SCALE, (TOTAL_ROWS, doc_rows.shape[1]))
    for n in range(word_sums.shape[0] // part_rows):
        word_sums[(n + 1) * part_rows - TOTAL_ROWS : (n + 1) * part_rows, :] = total
    near_rows = N_X_LO * part_rows
    start_row = N_Y * near_rows
    for out in send_out:
        leaving.append(leave(len(leaving), word_sums.at[pl.ds(start_row, out.shape[0])], out))
        start_row += out.shape[0]
    start_row = 0
    for out in keep_out:
        leaving.append(leave(len(leaving), word_sums.at[pl.ds(start_row, out.shape[0])], out))
        start_row += out.shape[0]
    for copy in leaving:
        copy.wait()


def run_tiles(
    pair_list, own_load, docs_index, vocab_index, doc_topics, word_topics, weight_table, counts_all
):
    slots = pair_list.shape[-1]
    tile_docs, tile_words = counts_all.shape[1:]
    topics = doc_topics.shape[1]
    doc_blocks = doc_topics.shape[0] // tile_docs
    items = slots + doc_blocks + AT_ONCE
    doc_part = jax.ShapeDtypeStruct((doc_topics.shape[0] // N_Z, topics), jnp.float32)
    word_rows = word_topics.shape[0] // (N_CORE * N_Y) + N_X_LO * TOTAL_ROWS
    first_part = jax.ShapeDtypeStruct((word_rows, topics), jnp.float32)
    later_part = jax.ShapeDtypeStruct(((N_Y - 1) * word_rows, topics), jnp.float32)
    smem = pl.BlockSpec(memory_space=pltpu.SMEM)
    hbm = pl.BlockSpec(memory_space=pl.ANY)
    return pl.pallas_call(
        tiles_kernel,
        out_shape=(
            (doc_part,) * N_Z,
            (first_part, later_part),
            (first_part, later_part),
        ),
        in_specs=[hbm] + [smem] * 3 + [hbm] * 4,
        out_specs=((hbm,) * N_Z, (hbm,) * 2, (hbm,) * 2),
        scratch_shapes=[
            pltpu.SMEM(pair_list.shape[1:], jnp.int32),
            pltpu.VMEM(weight_table.shape, jnp.float32),
            pltpu.VMEM(doc_topics.shape, jnp.float32),
            pltpu.VMEM((N_CORE * N_Y * word_rows, topics), jnp.float32),
            pltpu.VMEM(doc_topics.shape, doc_topics.dtype),
            pltpu.VMEM(word_topics.shape, word_topics.dtype),
            pltpu.VMEM((SLOTS, 2, tile_docs, tile_words), counts_all.dtype),
            pltpu.SMEM((items,), jnp.int32),
            pltpu.SMEM((items,), jnp.int32),
            pltpu.SMEM((items,), jnp.int32),
            pltpu.SMEM((doc_blocks,), jnp.int32),
            pltpu.SemaphoreType.DMA((4,)),
            pltpu.SemaphoreType.DMA((SLOTS, 2)),
            pltpu.SemaphoreType.DMA((N_Z + 4,)),
        ],
        compiler_params=pltpu.CompilerParams(vmem_limit_bytes=48 << 20),
        name="tiles",
    )(
        pair_list,
        own_load,
        docs_index,
        vocab_index,
        doc_topics,
        word_topics,
        weight_table,
        counts_all,
    )


def moves(axis, size, move):
    return lambda value: lax.ppermute(value, axis, [(n, move(n) % size) for n in range(size)])


def to_half(value):
    return value.astype(jnp.float16)


def to_float(value):
    return value.astype(jnp.float32)


def on_device(doc_topics, word_topics, word_weights, tile_pairs, tile_counts, tile_load):
    n_docs, n_vocab = lax.axis_size("docs"), lax.axis_size("vocab")
    docs_index, vocab_index = lax.axis_index("docs"), lax.axis_index("vocab")
    x_lo = docs_index // N_CORE % N_X_LO
    z, x_hi = vocab_index // N_X_HI, vocab_index % N_X_HI
    to_core = moves("docs", n_docs, lambda n: n ^ 1)
    to_x_lo = moves("docs", n_docs, lambda n: n ^ N_CORE)
    y_up = moves("docs", n_docs, lambda n: n + N_X_LO * N_CORE)
    y_down = moves("docs", n_docs, lambda n: n - N_X_LO * N_CORE)
    to_x_hi = moves("vocab", n_vocab, lambda n: n ^ 1)
    z_up = moves("vocab", n_vocab, lambda n: n + N_X_HI)
    z_down = moves("vocab", n_vocab, lambda n: n - N_X_HI)

    counts_all = tile_counts[0, 0]
    tile_words = counts_all.shape[2]
    blocks = word_topics.shape[0] // tile_words
    weight_table = word_weights.reshape(blocks, tile_words)
    doc_parts, keep, send = run_tiles(
        tile_pairs,
        tile_load,
        docs_index.reshape(1),
        vocab_index.reshape(1),
        doc_topics,
        word_topics,
        weight_table,
        counts_all,
    )

    z_across = moves("vocab", n_vocab, lambda n: n + 2 * N_X_HI)
    meet = lambda *values: lax.optimization_barrier(values)
    near_rows = keep[0].shape[0]
    word_rows = near_rows // N_X_LO
    doc_rows = doc_parts[0].shape[0] // N_X_HI

    part = [piece * DOC_SCALE for piece in doc_parts]
    word_far = to_core(send[0])
    doc_up = z_up(to_half(part[2][:doc_rows]))
    doc_down = z_down(to_half(part[2][doc_rows:]))
    word_far, doc_up, doc_down = meet(word_far, doc_up, doc_down)

    far = (keep[0] + word_far) * WORD_SCALE
    word_up = y_up(to_half(far[:word_rows]))
    word_down = y_down(to_half(far[word_rows:]))
    near_far = to_core(send[1])
    doc_below = z_up(
        to_half(jnp.concatenate([part[1][:doc_rows] + to_float(doc_up), part[1][doc_rows:]]))
    )
    doc_above = z_down(
        to_half(jnp.concatenate([part[3][:doc_rows], part[3][doc_rows:] + to_float(doc_down)]))
    )
    word_up, word_down, near_far, doc_below, doc_above = meet(
        word_up, word_down, near_far, doc_below, doc_above
    )

    near = (keep[1] + near_far) * WORD_SCALE
    above, below, here = near[:near_rows], near[near_rows : 2 * near_rows], near[2 * near_rows :]
    word_below = y_up(
        to_half(jnp.concatenate([above[:word_rows] + to_float(word_up), above[word_rows:]]))
    )
    word_above = y_down(
        to_half(jnp.concatenate([below[:word_rows], below[word_rows:] + to_float(word_down)]))
    )
    doc_pair = part[0] + to_float(doc_below) + to_float(doc_above)
    doc_mine = lax.dynamic_slice_in_dim(doc_pair, x_hi * doc_rows, doc_rows, 0)
    doc_other = lax.dynamic_slice_in_dim(doc_pair, (1 - x_hi) * doc_rows, doc_rows, 0)
    doc_sums = (doc_mine + to_float(to_x_hi(to_half(doc_other)))) / DOC_SCALE
    own_docs = lax.dynamic_slice_in_dim(doc_topics, vocab_index * doc_rows, doc_rows, 0)
    doc_scaled = own_docs.astype(jnp.float32) * doc_sums + prior_doc
    doc_block = to_half(
        doc_topics.shape[1] * doc_scaled / jnp.sum(doc_scaled, axis=1, keepdims=True)
    )
    doc_far = to_x_hi(doc_block)
    word_below, word_above, doc_block, doc_far = meet(word_below, word_above, doc_block, doc_far)

    word_pair = here + to_float(word_below) + to_float(word_above)
    word_mine = lax.dynamic_slice_in_dim(word_pair, x_lo * word_rows, word_rows, 0)
    word_other = lax.dynamic_slice_in_dim(word_pair, (1 - x_lo) * word_rows, word_rows, 0)
    word_far = to_x_lo(to_half(word_other))
    doc_here = jnp.concatenate(
        [
            jnp.where(x_hi == 0, doc_block, doc_far),
            jnp.where(x_hi == 0, doc_far, doc_block),
        ]
    )
    doc_below, doc_above = z_up(doc_here), z_down(doc_here)
    word_far, doc_below, doc_above = meet(word_far, doc_below, doc_above)

    low_across, high_across = z_up(doc_below[:doc_rows]), z_down(doc_above[doc_rows:])
    row_count = word_topics.shape[0] // n_docs
    word_sums = (word_mine + to_float(word_far)) / WORD_SCALE
    column = word_sums[row_count : row_count + 1] / TOTAL_SCALE
    column = column + to_x_hi(column)
    column = column + z_up(column) + z_down(column) + z_across(column)
    vocab_total = word_topics.shape[0] * n_vocab
    own_words = lax.dynamic_slice_in_dim(word_topics, docs_index * row_count, row_count, 0)
    word_scaled = own_words.astype(jnp.float32) * word_sums[:row_count] + prior_word
    word_next = vocab_total * word_scaled / (column + vocab_total * prior_word)
    by_step = (doc_here, doc_above, jnp.concatenate([low_across, high_across]), doc_below)
    doc_next = jnp.concatenate(
        [to_float(lax.select_n((place - z) % N_Z, *by_step)) for place in range(N_Z)]
    )
    return (doc_next, word_next)


def solution(mesh):
    placed = (
        P("docs", None),
        P("vocab", None),
        P("vocab"),
        P("docs", "vocab", None),
        P("docs", "vocab", None, None, None),
        P("docs", "vocab"),
    )
    return jax.shard_map(
        on_device,
        mesh=mesh,
        in_specs=placed,
        out_specs=(P("docs", None), P(("vocab", "docs"), None)),
        check_vma=False,
    )
```

```python
import jax
import jax.numpy as jnp
from jax import lax
from jax.experimental import pallas as pl
from jax.experimental.pallas import tpu as pltpu
from jax.sharding import PartitionSpec as P

prior_doc = 0.5
prior_word = 0.01
SLOTS = 16
AT_ONCE = 4
N_Y, N_X_LO, N_CORE = 4, 2, 2
N_Z, N_X_HI = 4, 2
WORD_SCALE = 2.0**-7
DOC_SCALE = 2.0**-8
TOTAL_SCALE = 2.0**-6
TOTAL_ROWS = 16


def tiles_kernel(
    pairs_hbm,
    load_ref,
    docs_index_ref,
    vocab_index_ref,
    doc_hbm,
    word_hbm,
    weights_hbm,
    counts_hbm,
    doc_parts_out,
    keep_out,
    send_out,
    pairs_ref,
    weights_ref,
    doc_sums,
    word_sums,
    doc_rows,
    word_rows,
    counts_buf,
    first_slot,
    second_slot,
    item_doc,
    pending,
    topics_sem,
    counts_sem,
    sums_sem,
):
    tile_docs, tile_words = counts_hbm.shape[1:]
    blocks = word_hbm.shape[0] // tile_words
    doc_blocks = doc_hbm.shape[0] // tile_docs
    load = load_ref[0, 0]
    y, own_core = docs_index_ref[0] // (N_X_LO * N_CORE), lax.rem(docs_index_ref[0], N_CORE)
    z = vocab_index_ref[0] // N_X_HI
    dest_blocks = blocks // (N_Y * N_X_LO * N_CORE)

    half_docs = tile_docs // N_X_HI
    half_rows = half_docs + TOTAL_ROWS

    def word_place(block):
        dest = block // dest_blocks
        core = lax.rem(dest, N_CORE)
        x_lo = lax.rem(dest // N_CORE, N_X_LO)
        step = lax.rem(dest // (N_CORE * N_X_LO) - y + N_Y, N_Y)
        other = jnp.where(core == own_core, 0, 1)
        place = jnp.where(step == 0, 3, jnp.where(step == 2, 0, (step + 1) // 2))
        part = (other * N_Y + place) * N_X_LO + x_lo
        return (part * dest_blocks + lax.rem(block, dest_blocks)) * tile_words

    doc_copy = pltpu.make_async_copy(doc_hbm, doc_rows, topics_sem.at[0])
    word_copy = pltpu.make_async_copy(word_hbm, word_rows, topics_sem.at[1])
    pairs_copy = pltpu.make_async_copy(pairs_hbm.at[0], pairs_ref, topics_sem.at[2])
    weights_copy = pltpu.make_async_copy(weights_hbm, weights_ref, topics_sem.at[3])
    pairs_copy.start()
    doc_copy.start()
    word_copy.start()
    weights_copy.start()

    for b in range(doc_blocks):
        pending[b] = -1

    pairs_copy.wait()

    def sort_slot(s, made):
        b = pairs_ref[0, s] // blocks
        waiting = pending[b]
        first_slot[made] = waiting
        second_slot[made] = s
        item_doc[made] = b
        pending[b] = jnp.where(waiting >= 0, -1, s)
        return made + jnp.where(waiting >= 0, 1, 0)

    made = lax.fori_loop(0, load, sort_slot, 0)
    for b in range(doc_blocks):
        waiting = pending[b]
        first_slot[made] = waiting
        second_slot[made] = -1
        item_doc[made] = b
        made = made + jnp.where(waiting >= 0, 1, 0)

    def pad_item(n, carry):
        first_slot[made + n] = -1
        second_slot[made + n] = -1
        item_doc[made + n] = 0
        return carry

    lax.fori_loop(0, AT_ONCE - 1, pad_item, 0)
    rounds = (made + AT_ONCE - 1) // AT_ONCE

    def copies(item):
        ring = lax.rem(item, SLOTS)
        return [
            pltpu.make_async_copy(
                counts_hbm.at[jnp.maximum(slots[item], 0)],
                counts_buf.at[ring, n],
                counts_sem.at[ring, n],
            )
            for n, slots in enumerate((first_slot, second_slot))
        ]

    def start(n):
        @pl.when(n < rounds)
        def _():
            for item in range(AT_ONCE):
                for copy in copies(n * AT_ONCE + item):
                    copy.start()

    for ahead in range(SLOTS // AT_ONCE - 1):
        start(ahead)

    doc_sums[...] = jnp.zeros_like(doc_sums)
    word_sums[...] = jnp.zeros_like(word_sums)
    doc_copy.wait()
    word_copy.wait()
    weights_copy.wait()

    def load_item(item):
        doc_at = pl.multiple_of(item_doc[item] * tile_docs, tile_docs)
        docs = doc_rows[pl.ds(doc_at, tile_docs), :]
        words, weight, counts, word_blocks = [], [], [], []
        for n, slots in enumerate((first_slot, second_slot)):
            block = lax.rem(pairs_ref[0, jnp.maximum(slots[item], 0)], blocks)
            word_at = pl.multiple_of(block * tile_words, tile_words)
            words.append(word_rows[pl.ds(word_at, tile_words), :])
            live = jnp.where(slots[item] >= 0, 1.0, 0.0)
            weight.append(weights_ref[pl.ds(block, 1), :] * live)
            counts.append(counts_buf[lax.rem(item, SLOTS), n])
            word_blocks.append(block)
        words = jnp.concatenate(words, axis=0)
        weight = jnp.concatenate(weight, axis=1)
        counts = jnp.concatenate(counts, axis=1)
        return docs, words, weight, counts, word_blocks

    def count_ratio(docs, words, weight, counts):
        predicted = lax.dot_general(
            docs, words, (((1,), (1,)), ((), ())), preferred_element_type=jnp.float32
        )
        weighted = (counts.astype(jnp.float32) * weight).astype(jnp.bfloat16)
        return (weighted.astype(jnp.float32) / predicted).astype(jnp.bfloat16)

    def add_terms(item, ratio, docs, words, word_blocks):
        doc_step = lax.rem(item_doc[item] - z + N_Z, N_Z)
        doc_terms = jnp.dot(ratio, words, preferred_element_type=jnp.float32)
        for half in range(N_X_HI):
            to = pl.multiple_of((doc_step * N_X_HI + half) * half_rows, TOTAL_ROWS)
            doc_sums[pl.ds(to, half_docs), :] += doc_terms[half * half_docs : (half + 1) * half_docs]
        terms = lax.dot_general(
            ratio, docs, (((0,), (0,)), ((), ())), preferred_element_type=jnp.float32
        )
        for n, block in enumerate(word_blocks):
            to = pl.multiple_of(word_place(block), tile_words)
            word_sums[pl.ds(to, tile_words), :] += terms[n * tile_words : (n + 1) * tile_words]

    def run_items(n, carry):
        start(n + SLOTS // AT_ONCE - 1)
        items = [n * AT_ONCE + item for item in range(AT_ONCE)]
        for item in items:
            for copy in copies(item):
                copy.wait()
        loaded = [load_item(item) for item in items]
        ratios = [count_ratio(*fields[:4]) for fields in loaded]
        for item, ratio, (docs, words, _, _, word_blocks) in zip(items, ratios, loaded):
            add_terms(item, ratio, docs, words, word_blocks)
        return carry

    lax.fori_loop(0, rounds, run_items, 0)

    def leave(n, source, target):
        copy = pltpu.make_async_copy(source, target, sums_sem.at[n])
        copy.start()
        return copy

    leaving = []
    start_row = N_Y * N_X_LO * dest_blocks * tile_words
    for out in send_out:
        leaving.append(leave(len(leaving), word_sums.at[pl.ds(start_row, out.shape[0])], out))
        start_row += out.shape[0]
    total = jnp.zeros((1, doc_rows.shape[1]), jnp.float32)
    for step in range(N_Z):
        for half in range(N_X_HI):
            at = pl.multiple_of(lax.rem(z + step, N_Z) * tile_docs + half * half_docs, half_docs)
            topics = doc_rows[pl.ds(at, half_docs), :].astype(jnp.float32)
            sums = doc_sums[pl.ds((step * N_X_HI + half) * half_rows, half_docs), :]
            total = total + jnp.sum(topics * sums, axis=0, keepdims=True)
    total = jnp.broadcast_to(total * TOTAL_SCALE, (TOTAL_ROWS, doc_rows.shape[1]))
    for n in range(N_Z * N_X_HI):
        doc_sums[(n + 1) * half_rows - TOTAL_ROWS : (n + 1) * half_rows, :] = total
    for step in range(N_Z):
        source = doc_sums.at[pl.ds(step * N_X_HI * half_rows, N_X_HI * half_rows)]
        leaving.append(leave(len(leaving), source, doc_parts_out[step]))
    start_row = 0
    for out in keep_out:
        leaving.append(leave(len(leaving), word_sums.at[pl.ds(start_row, out.shape[0])], out))
        start_row += out.shape[0]
    for copy in leaving:
        copy.wait()


def run_tiles(
    pair_list, own_load, docs_index, vocab_index, doc_topics, word_topics, weight_table, counts_all
):
    slots = pair_list.shape[-1]
    tile_docs, tile_words = counts_all.shape[1:]
    topics = doc_topics.shape[1]
    doc_blocks = doc_topics.shape[0] // tile_docs
    items = slots + doc_blocks + AT_ONCE
    doc_rows = doc_topics.shape[0] // N_Z + N_X_HI * TOTAL_ROWS
    doc_part = jax.ShapeDtypeStruct((doc_rows, topics), jnp.float32)
    word_rows = word_topics.shape[0] // (N_CORE * N_Y)
    first_part = jax.ShapeDtypeStruct((word_rows, topics), jnp.float32)
    later_part = jax.ShapeDtypeStruct(((N_Y - 1) * word_rows, topics), jnp.float32)
    smem = pl.BlockSpec(memory_space=pltpu.SMEM)
    source = pl.BlockSpec(memory_space=pltpu.HBM)
    hbm = pl.BlockSpec(memory_space=pl.ANY)
    return pl.pallas_call(
        tiles_kernel,
        out_shape=(
            (doc_part,) * N_Z,
            (first_part, later_part),
            (first_part, later_part),
        ),
        in_specs=[source] + [smem] * 3 + [source] * 4,
        out_specs=((hbm,) * N_Z, (hbm,) * 2, (hbm,) * 2),
        scratch_shapes=[
            pltpu.SMEM(pair_list.shape[1:], jnp.int32),
            pltpu.VMEM(weight_table.shape, jnp.float32),
            pltpu.VMEM((N_Z * doc_rows, topics), jnp.float32),
            pltpu.VMEM(word_topics.shape, jnp.float32),
            pltpu.VMEM(doc_topics.shape, doc_topics.dtype),
            pltpu.VMEM(word_topics.shape, word_topics.dtype),
            pltpu.VMEM((SLOTS, 2, tile_docs, tile_words), counts_all.dtype),
            pltpu.SMEM((items,), jnp.int32),
            pltpu.SMEM((items,), jnp.int32),
            pltpu.SMEM((items,), jnp.int32),
            pltpu.SMEM((doc_blocks,), jnp.int32),
            pltpu.SemaphoreType.DMA((4,)),
            pltpu.SemaphoreType.DMA((SLOTS, 2)),
            pltpu.SemaphoreType.DMA((N_Z + 4,)),
        ],
        compiler_params=pltpu.CompilerParams(vmem_limit_bytes=48 << 20),
        name="tiles",
    )(
        pair_list,
        own_load,
        docs_index,
        vocab_index,
        doc_topics,
        word_topics,
        weight_table,
        counts_all,
    )


def moves(axis, size, move):
    return lambda value: lax.ppermute(value, axis, [(n, move(n) % size) for n in range(size)])


def to_half(value):
    return value.astype(jnp.float16)


def to_float(value):
    return value.astype(jnp.float32)


def rows_around(value, before, after):
    return lax.pad(value, jnp.zeros((), value.dtype), ((before, after, 0), (0, 0, 0)))


def on_device(doc_topics, word_topics, word_weights, tile_pairs, tile_counts, tile_load):
    n_docs, n_vocab = lax.axis_size("docs"), lax.axis_size("vocab")
    docs_index, vocab_index = lax.axis_index("docs"), lax.axis_index("vocab")
    x_lo = docs_index // N_CORE % N_X_LO
    z, x_hi = vocab_index // N_X_HI, vocab_index % N_X_HI
    to_core = moves("docs", n_docs, lambda n: n ^ 1)
    to_x_lo = moves("docs", n_docs, lambda n: n ^ N_CORE)
    y_up = moves("docs", n_docs, lambda n: n + N_X_LO * N_CORE)
    y_down = moves("docs", n_docs, lambda n: n - N_X_LO * N_CORE)
    y_pair = moves("docs", n_docs, lambda n: n ^ (N_X_LO * N_CORE))
    y_cross = moves("docs", n_docs, lambda n: n ^ ((N_Y - 1) * N_X_LO * N_CORE))
    to_x_hi = moves("vocab", n_vocab, lambda n: n ^ 1)
    z_up = moves("vocab", n_vocab, lambda n: n + N_X_HI)
    z_down = moves("vocab", n_vocab, lambda n: n - N_X_HI)

    counts_all = tile_counts[0, 0]
    tile_words = counts_all.shape[2]
    blocks = word_topics.shape[0] // tile_words
    weight_table = word_weights.reshape(blocks, tile_words)
    doc_parts, keep, send = run_tiles(
        tile_pairs,
        tile_load,
        docs_index.reshape(1),
        vocab_index.reshape(1),
        doc_topics,
        word_topics,
        weight_table,
        counts_all,
    )

    meet = lambda *values: lax.optimization_barrier(values)
    near_rows = keep[0].shape[0]
    word_rows = near_rows // N_X_LO
    doc_rows = doc_parts[0].shape[0] // N_X_HI

    part = [piece * DOC_SCALE for piece in doc_parts]
    word_far = to_core(send[0])
    doc_up = z_up(to_half(part[2][:doc_rows]))
    doc_down = z_down(to_half(part[2][doc_rows:]))
    word_far, doc_up, doc_down = meet(word_far, doc_up, doc_down)

    far = (keep[0] + word_far) * WORD_SCALE
    word_up = y_up(to_half(far[:word_rows]))
    word_down = y_down(to_half(far[word_rows:]))
    near_far = to_core(send[1])
    doc_below = z_up(to_half(part[1] + rows_around(to_float(doc_up), 0, doc_rows)))
    doc_above = z_down(to_half(part[3] + rows_around(to_float(doc_down), doc_rows, 0)))
    word_up, word_down, near_far, doc_below, doc_above = meet(
        word_up, word_down, near_far, doc_below, doc_above
    )

    above = (keep[1][:near_rows] + near_far[:near_rows]) * WORD_SCALE
    below = (
        keep[1][near_rows : 2 * near_rows] + near_far[near_rows : 2 * near_rows]
    ) * WORD_SCALE
    word_below = y_up(to_half(above + rows_around(to_float(word_up), 0, word_rows)))
    word_above = y_down(to_half(below + rows_around(to_float(word_down), word_rows, 0)))

    def doc_half(which):
        rows = [
            lax.dynamic_slice_in_dim(value, which * doc_rows, doc_rows, 0)
            for value in (doc_parts[0], doc_below, doc_above)
        ]
        return rows[0] * DOC_SCALE + to_float(rows[1]) + to_float(rows[2])

    doc_mine, doc_other = doc_half(x_hi), doc_half(1 - x_hi)
    doc_sums = (doc_mine + to_float(to_x_hi(to_half(doc_other)))) / DOC_SCALE
    own_rows = doc_topics.shape[0] // n_vocab
    own_docs = lax.dynamic_slice_in_dim(doc_topics, vocab_index * own_rows, own_rows, 0)
    doc_scaled = own_docs.astype(jnp.float32) * doc_sums[:own_rows] + prior_doc
    doc_block = to_half(
        doc_topics.shape[1] * doc_scaled / jnp.sum(doc_scaled, axis=1, keepdims=True)
    )
    doc_far = to_x_hi(doc_block)
    column = doc_sums[own_rows : own_rows + 1] / TOTAL_SCALE
    column = column + to_core(column)
    column = column + y_pair(column)
    word_below, word_above, doc_block, doc_far, column = meet(
        word_below, word_above, doc_block, doc_far, column
    )

    def word_half(which):
        at = which * word_rows
        here = lax.dynamic_slice_in_dim(keep[1], 2 * near_rows + at, word_rows, 0)
        far = lax.dynamic_slice_in_dim(near_far, 2 * near_rows + at, word_rows, 0)
        below = lax.dynamic_slice_in_dim(word_below, at, word_rows, 0)
        above = lax.dynamic_slice_in_dim(word_above, at, word_rows, 0)
        return (here + far) * WORD_SCALE + to_float(below) + to_float(above)

    word_far = to_x_lo(to_half(word_half(1 - x_lo)))
    doc_here = rows_around(jnp.where(x_hi == 0, doc_block, doc_far), 0, own_rows) + rows_around(
        jnp.where(x_hi == 0, doc_far, doc_block), own_rows, 0
    )
    doc_below, doc_above = z_up(doc_here), z_down(doc_here)
    column = column + y_cross(column)
    column = column + to_x_lo(column)
    word_far, doc_below, doc_above, column = meet(word_far, doc_below, doc_above, column)

    doc_across = z_up(doc_below)
    doc_next = jnp.zeros(doc_topics.shape, jnp.float32)
    for step, value in ((0, doc_here), (1, doc_above), (3, doc_below), (2, doc_across)):
        at = (z + step) % N_Z * (N_X_HI * own_rows)
        doc_next = lax.dynamic_update_slice_in_dim(doc_next, to_float(value), at, 0)
    row_count = word_topics.shape[0] // n_docs
    word_sums = (word_half(x_lo) + to_float(word_far)) / WORD_SCALE
    vocab_total = word_topics.shape[0] * n_vocab
    own_words = lax.dynamic_slice_in_dim(word_topics, docs_index * row_count, row_count, 0)
    word_scaled = own_words.astype(jnp.float32) * word_sums + prior_word
    word_next = vocab_total * word_scaled / (column + vocab_total * prior_word)
    return (doc_next, word_next)


def solution(mesh):
    placed = (
        P("docs", None),
        P("vocab", None),
        P("vocab"),
        P("docs", "vocab", None),
        P("docs", "vocab", None, None, None),
        P("docs", "vocab"),
    )
    return jax.shard_map(
        on_device,
        mesh=mesh,
        in_specs=placed,
        out_specs=(P("docs", None), P(("vocab", "docs"), None)),
        check_vma=False,
    )
```

```python
import jax
import jax.numpy as jnp
from jax import lax
from jax.experimental import pallas as pl
from jax.experimental.pallas import tpu as pltpu
from jax.sharding import PartitionSpec as P

prior_doc = 0.5
prior_word = 0.01
SLOTS = 16
AT_ONCE = 4
N_Y, N_X_LO, N_CORE = 4, 2, 2
N_Z, N_X_HI = 4, 2
WORD_SCALE = 2.0**-7
DOC_SCALE = 2.0**-8
TOTAL_SCALE = 2.0**-6
TOTAL_ROWS = 16


def tiles_kernel(
    pairs_hbm,
    load_ref,
    docs_index_ref,
    vocab_index_ref,
    doc_hbm,
    word_hbm,
    weights_hbm,
    counts_hbm,
    doc_parts_out,
    keep_out,
    send_out,
    pairs_ref,
    weights_ref,
    doc_sums,
    word_sums,
    doc_rows,
    word_rows,
    counts_buf,
    first_slot,
    second_slot,
    item_doc,
    pending,
    topics_sem,
    counts_sem,
    sums_sem,
):
    tile_docs, tile_words = counts_hbm.shape[1:]
    blocks = word_hbm.shape[0] // tile_words
    doc_blocks = doc_hbm.shape[0] // tile_docs
    load = load_ref[0, 0]
    y, own_core = docs_index_ref[0] // (N_X_LO * N_CORE), lax.rem(docs_index_ref[0], N_CORE)
    z = vocab_index_ref[0] // N_X_HI
    dest_blocks = blocks // (N_Y * N_X_LO * N_CORE)

    half_docs = tile_docs // N_X_HI
    half_rows = half_docs + TOTAL_ROWS

    def word_place(block):
        dest = block // dest_blocks
        core = lax.rem(dest, N_CORE)
        x_lo = lax.rem(dest // N_CORE, N_X_LO)
        step = lax.rem(dest // (N_CORE * N_X_LO) - y + N_Y, N_Y)
        other = jnp.where(core == own_core, 0, 1)
        place = jnp.where(step == 0, 3, jnp.where(step == 2, 0, (step + 1) // 2))
        part = (other * N_Y + place) * N_X_LO + x_lo
        return (part * dest_blocks + lax.rem(block, dest_blocks)) * tile_words

    doc_copy = pltpu.make_async_copy(doc_hbm, doc_rows, topics_sem.at[0])
    word_copy = pltpu.make_async_copy(word_hbm, word_rows, topics_sem.at[1])
    pairs_copy = pltpu.make_async_copy(pairs_hbm.at[0], pairs_ref, topics_sem.at[2])
    weights_copy = pltpu.make_async_copy(weights_hbm, weights_ref, topics_sem.at[3])
    pairs_copy.start()
    doc_copy.start()
    word_copy.start()
    weights_copy.start()

    for b in range(doc_blocks):
        pending[b] = -1

    pairs_copy.wait()

    def sort_slot(s, made):
        b = pairs_ref[0, s] // blocks
        waiting = pending[b]
        first_slot[made] = waiting
        second_slot[made] = s
        item_doc[made] = b
        pending[b] = jnp.where(waiting >= 0, -1, s)
        return made + jnp.where(waiting >= 0, 1, 0)

    made = lax.fori_loop(0, load, sort_slot, 0)
    for b in range(doc_blocks):
        waiting = pending[b]
        first_slot[made] = waiting
        second_slot[made] = -1
        item_doc[made] = b
        made = made + jnp.where(waiting >= 0, 1, 0)

    def pad_item(n, carry):
        first_slot[made + n] = -1
        second_slot[made + n] = -1
        item_doc[made + n] = 0
        return carry

    lax.fori_loop(0, AT_ONCE - 1, pad_item, 0)
    rounds = (made + AT_ONCE - 1) // AT_ONCE

    def copies(item):
        ring = lax.rem(item, SLOTS)
        return [
            pltpu.make_async_copy(
                counts_hbm.at[jnp.maximum(slots[item], 0)],
                counts_buf.at[ring, n],
                counts_sem.at[ring, n],
            )
            for n, slots in enumerate((first_slot, second_slot))
        ]

    def start(n):
        @pl.when(n < rounds)
        def _():
            for item in range(AT_ONCE):
                for copy in copies(n * AT_ONCE + item):
                    copy.start()

    for ahead in range(SLOTS // AT_ONCE - 1):
        start(ahead)

    doc_sums[...] = jnp.zeros_like(doc_sums)
    word_sums[...] = jnp.zeros_like(word_sums)
    doc_copy.wait()
    word_copy.wait()
    weights_copy.wait()

    def load_item(item):
        doc_at = pl.multiple_of(item_doc[item] * tile_docs, tile_docs)
        docs = doc_rows[pl.ds(doc_at, tile_docs), :]
        words, weight, counts, word_blocks = [], [], [], []
        for n, slots in enumerate((first_slot, second_slot)):
            block = lax.rem(pairs_ref[0, jnp.maximum(slots[item], 0)], blocks)
            word_at = pl.multiple_of(block * tile_words, tile_words)
            words.append(word_rows[pl.ds(word_at, tile_words), :])
            live = jnp.where(slots[item] >= 0, 1.0, 0.0)
            weight.append(weights_ref[pl.ds(block, 1), :] * live)
            counts.append(counts_buf[lax.rem(item, SLOTS), n])
            word_blocks.append(block)
        words = jnp.concatenate(words, axis=0)
        weight = jnp.concatenate(weight, axis=1)
        counts = jnp.concatenate(counts, axis=1)
        return docs, words, weight, counts, word_blocks

    def count_ratio(docs, words, weight, counts):
        predicted = lax.dot_general(
            docs, words, (((1,), (1,)), ((), ())), preferred_element_type=jnp.float32
        )
        weighted = (counts.astype(jnp.float32) * weight).astype(jnp.bfloat16)
        return (weighted.astype(jnp.float32) / predicted).astype(jnp.bfloat16)

    def add_terms(item, ratio, docs, words, word_blocks):
        doc_step = lax.rem(item_doc[item] - z + N_Z, N_Z)
        doc_terms = jnp.dot(ratio, words, preferred_element_type=jnp.float32)
        for half in range(N_X_HI):
            to = pl.multiple_of((doc_step * N_X_HI + half) * half_rows, TOTAL_ROWS)
            doc_sums[pl.ds(to, half_docs), :] += doc_terms[half * half_docs : (half + 1) * half_docs]
        terms = lax.dot_general(
            ratio, docs, (((0,), (0,)), ((), ())), preferred_element_type=jnp.float32
        )
        for n, block in enumerate(word_blocks):
            to = pl.multiple_of(word_place(block), tile_words)
            word_sums[pl.ds(to, tile_words), :] += terms[n * tile_words : (n + 1) * tile_words]

    def run_items(n, carry):
        start(n + SLOTS // AT_ONCE - 1)
        items = [n * AT_ONCE + item for item in range(AT_ONCE)]
        for item in items:
            for copy in copies(item):
                copy.wait()
        loaded = [load_item(item) for item in items]
        ratios = [count_ratio(*fields[:4]) for fields in loaded]
        for item, ratio, (docs, words, _, _, word_blocks) in zip(items, ratios, loaded):
            add_terms(item, ratio, docs, words, word_blocks)
        return carry

    lax.fori_loop(0, rounds, run_items, 0)

    def leave(n, source, target):
        copy = pltpu.make_async_copy(source, target, sums_sem.at[n])
        copy.start()
        return copy

    leaving = []
    start_row = N_Y * N_X_LO * dest_blocks * tile_words
    for out in send_out:
        leaving.append(leave(len(leaving), word_sums.at[pl.ds(start_row, out.shape[0])], out))
        start_row += out.shape[0]
    total = jnp.zeros((1, doc_rows.shape[1]), jnp.float32)
    for step in range(N_Z):
        for half in range(N_X_HI):
            at = pl.multiple_of(lax.rem(z + step, N_Z) * tile_docs + half * half_docs, half_docs)
            topics = doc_rows[pl.ds(at, half_docs), :].astype(jnp.float32)
            sums = doc_sums[pl.ds((step * N_X_HI + half) * half_rows, half_docs), :]
            total = total + jnp.sum(topics * sums, axis=0, keepdims=True)
    total = jnp.broadcast_to(total * TOTAL_SCALE, (TOTAL_ROWS, doc_rows.shape[1]))
    for n in range(N_Z * N_X_HI):
        doc_sums[(n + 1) * half_rows - TOTAL_ROWS : (n + 1) * half_rows, :] = total
    for step in range(N_Z):
        source = doc_sums.at[pl.ds(step * N_X_HI * half_rows, N_X_HI * half_rows)]
        leaving.append(leave(len(leaving), source, doc_parts_out[step]))
    start_row = 0
    for out in keep_out:
        leaving.append(leave(len(leaving), word_sums.at[pl.ds(start_row, out.shape[0])], out))
        start_row += out.shape[0]
    for copy in leaving:
        copy.wait()


def in_hbm(value):
    return pltpu.with_memory_space_constraint(value, pltpu.HBM)


def run_tiles(
    pair_list, own_load, docs_index, vocab_index, doc_topics, word_topics, weight_table, counts_all
):
    slots = pair_list.shape[-1]
    tile_docs, tile_words = counts_all.shape[1:]
    topics = doc_topics.shape[1]
    doc_blocks = doc_topics.shape[0] // tile_docs
    items = slots + doc_blocks + AT_ONCE
    doc_rows = doc_topics.shape[0] // N_Z + N_X_HI * TOTAL_ROWS
    doc_part = jax.ShapeDtypeStruct((doc_rows, topics), jnp.float32)
    word_rows = word_topics.shape[0] // (N_CORE * N_Y)
    first_part = jax.ShapeDtypeStruct((word_rows, topics), jnp.float32)
    later_part = jax.ShapeDtypeStruct(((N_Y - 1) * word_rows, topics), jnp.float32)
    smem = pl.BlockSpec(memory_space=pltpu.SMEM)
    source = pl.BlockSpec(memory_space=pltpu.HBM)
    hbm = pl.BlockSpec(memory_space=pl.ANY)
    return pl.pallas_call(
        tiles_kernel,
        out_shape=(
            (doc_part,) * N_Z,
            (first_part, later_part),
            (first_part, later_part),
        ),
        in_specs=[source] + [smem] * 3 + [source] * 4,
        out_specs=((hbm,) * N_Z, (hbm,) * 2, (hbm,) * 2),
        scratch_shapes=[
            pltpu.SMEM(pair_list.shape[1:], jnp.int32),
            pltpu.VMEM(weight_table.shape, jnp.float32),
            pltpu.VMEM((N_Z * doc_rows, topics), jnp.float32),
            pltpu.VMEM(word_topics.shape, jnp.float32),
            pltpu.VMEM(doc_topics.shape, doc_topics.dtype),
            pltpu.VMEM(word_topics.shape, word_topics.dtype),
            pltpu.VMEM((SLOTS, 2, tile_docs, tile_words), counts_all.dtype),
            pltpu.SMEM((items,), jnp.int32),
            pltpu.SMEM((items,), jnp.int32),
            pltpu.SMEM((items,), jnp.int32),
            pltpu.SMEM((doc_blocks,), jnp.int32),
            pltpu.SemaphoreType.DMA((4,)),
            pltpu.SemaphoreType.DMA((SLOTS, 2)),
            pltpu.SemaphoreType.DMA((N_Z + 4,)),
        ],
        compiler_params=pltpu.CompilerParams(vmem_limit_bytes=48 << 20),
        name="tiles",
    )(
        in_hbm(pair_list),
        own_load,
        docs_index,
        vocab_index,
        in_hbm(doc_topics),
        word_topics,
        in_hbm(weight_table),
        counts_all,
    )


def moves(axis, size, move):
    return lambda value: lax.ppermute(value, axis, [(n, move(n) % size) for n in range(size)])


def to_half(value):
    return value.astype(jnp.float16)


def to_float(value):
    return value.astype(jnp.float32)


def rows_around(value, before, after):
    return lax.pad(value, jnp.zeros((), value.dtype), ((before, after, 0), (0, 0, 0)))


def on_device(doc_topics, word_topics, word_weights, tile_pairs, tile_counts, tile_load):
    n_docs, n_vocab = lax.axis_size("docs"), lax.axis_size("vocab")
    docs_index, vocab_index = lax.axis_index("docs"), lax.axis_index("vocab")
    x_lo = docs_index // N_CORE % N_X_LO
    z, x_hi = vocab_index // N_X_HI, vocab_index % N_X_HI
    to_core = moves("docs", n_docs, lambda n: n ^ 1)
    to_x_lo = moves("docs", n_docs, lambda n: n ^ N_CORE)
    y_up = moves("docs", n_docs, lambda n: n + N_X_LO * N_CORE)
    y_down = moves("docs", n_docs, lambda n: n - N_X_LO * N_CORE)
    y_pair = moves("docs", n_docs, lambda n: n ^ (N_X_LO * N_CORE))
    y_cross = moves("docs", n_docs, lambda n: n ^ ((N_Y - 1) * N_X_LO * N_CORE))
    to_x_hi = moves("vocab", n_vocab, lambda n: n ^ 1)
    z_up = moves("vocab", n_vocab, lambda n: n + N_X_HI)
    z_down = moves("vocab", n_vocab, lambda n: n - N_X_HI)

    counts_all = tile_counts[0, 0]
    tile_words = counts_all.shape[2]
    blocks = word_topics.shape[0] // tile_words
    weight_table = word_weights.reshape(blocks, tile_words)
    doc_parts, keep, send = run_tiles(
        tile_pairs,
        tile_load,
        docs_index.reshape(1),
        vocab_index.reshape(1),
        doc_topics,
        word_topics,
        weight_table,
        counts_all,
    )

    meet = lambda *values: lax.optimization_barrier(values)
    near_rows = keep[0].shape[0]
    word_rows = near_rows // N_X_LO
    doc_rows = doc_parts[0].shape[0] // N_X_HI

    part = [piece * DOC_SCALE for piece in doc_parts]
    word_far = to_core(send[0])
    doc_up = z_up(to_half(part[2][:doc_rows]))
    doc_down = z_down(to_half(part[2][doc_rows:]))
    word_far, doc_up, doc_down = meet(word_far, doc_up, doc_down)

    far = (keep[0] + word_far) * WORD_SCALE
    word_up = y_up(to_half(far[:word_rows]))
    word_down = y_down(to_half(far[word_rows:]))
    near_far = to_core(send[1])
    doc_below = z_up(to_half(part[1] + rows_around(to_float(doc_up), 0, doc_rows)))
    doc_above = z_down(to_half(part[3] + rows_around(to_float(doc_down), doc_rows, 0)))
    word_up, word_down, near_far, doc_below, doc_above = meet(
        word_up, word_down, near_far, doc_below, doc_above
    )

    above = (keep[1][:near_rows] + near_far[:near_rows]) * WORD_SCALE
    below = (
        keep[1][near_rows : 2 * near_rows] + near_far[near_rows : 2 * near_rows]
    ) * WORD_SCALE
    word_below = y_up(to_half(above + rows_around(to_float(word_up), 0, word_rows)))
    word_above = y_down(to_half(below + rows_around(to_float(word_down), word_rows, 0)))

    def doc_half(which):
        rows = [
            lax.dynamic_slice_in_dim(value, which * doc_rows, doc_rows, 0)
            for value in (doc_parts[0], doc_below, doc_above)
        ]
        return rows[0] * DOC_SCALE + to_float(rows[1]) + to_float(rows[2])

    doc_mine, doc_other = doc_half(x_hi), doc_half(1 - x_hi)
    doc_sums = (doc_mine + to_float(to_x_hi(to_half(doc_other)))) / DOC_SCALE
    own_rows = doc_topics.shape[0] // n_vocab
    own_docs = lax.dynamic_slice_in_dim(doc_topics, vocab_index * own_rows, own_rows, 0)
    doc_scaled = own_docs.astype(jnp.float32) * doc_sums[:own_rows] + prior_doc
    doc_block = to_half(
        doc_topics.shape[1] * doc_scaled / jnp.sum(doc_scaled, axis=1, keepdims=True)
    )
    doc_far = to_x_hi(doc_block)
    column = doc_sums[own_rows : own_rows + 1] / TOTAL_SCALE
    column = column + to_core(column)
    column = column + to_x_lo(column)
    word_below, word_above, doc_block, doc_far, column = meet(
        word_below, word_above, doc_block, doc_far, column
    )

    def word_half(which):
        at = which * word_rows
        here = lax.dynamic_slice_in_dim(keep[1], 2 * near_rows + at, word_rows, 0)
        far = lax.dynamic_slice_in_dim(near_far, 2 * near_rows + at, word_rows, 0)
        below = lax.dynamic_slice_in_dim(word_below, at, word_rows, 0)
        above = lax.dynamic_slice_in_dim(word_above, at, word_rows, 0)
        return (here + far) * WORD_SCALE + to_float(below) + to_float(above)

    word_far = to_x_lo(to_half(word_half(1 - x_lo)))
    doc_here = rows_around(jnp.where(x_hi == 0, doc_block, doc_far), 0, own_rows) + rows_around(
        jnp.where(x_hi == 0, doc_far, doc_block), own_rows, 0
    )
    doc_below, doc_above = z_up(doc_here), z_down(doc_here)
    column = column + y_pair(column)
    word_far, doc_below, doc_above, column = meet(word_far, doc_below, doc_above, column)

    doc_across = z_up(doc_below)
    doc_next = jnp.zeros(doc_topics.shape, jnp.float32)
    for step, value in ((0, doc_here), (1, doc_above), (3, doc_below), (2, doc_across)):
        at = (z + step) % N_Z * (N_X_HI * own_rows)
        doc_next = lax.dynamic_update_slice_in_dim(doc_next, to_float(value), at, 0)
    column = column + y_cross(column)
    row_count = word_topics.shape[0] // n_docs
    word_sums = (word_half(x_lo) + to_float(word_far)) / WORD_SCALE
    vocab_total = word_topics.shape[0] * n_vocab
    own_words = lax.dynamic_slice_in_dim(word_topics, docs_index * row_count, row_count, 0)
    word_scaled = own_words.astype(jnp.float32) * word_sums + prior_word
    word_next = vocab_total * word_scaled / (column + vocab_total * prior_word)
    return (doc_next, word_next)


def solution(mesh):
    placed = (
        P("docs", None),
        P("vocab", None),
        P("vocab"),
        P("docs", "vocab", None),
        P("docs", "vocab", None, None, None),
        P("docs", "vocab"),
    )
    return jax.shard_map(
        on_device,
        mesh=mesh,
        in_specs=placed,
        out_specs=(P("docs", None), P(("vocab", "docs"), None)),
        check_vma=False,
    )
```

```python
import jax
import jax.numpy as jnp
from jax import lax
from jax.experimental import pallas as pl
from jax.experimental.pallas import tpu as pltpu
from jax.sharding import PartitionSpec as P

prior_doc = 0.5
prior_word = 0.01
WIDE = 4
SLOTS = 8
AT_ONCE = 2
N_Y, N_X_LO, N_CORE = 4, 2, 2
N_Z, N_X_HI = 4, 2
WORD_SCALE = 2.0**-7
DOC_SCALE = 2.0**-8
TOTAL_SCALE = 2.0**-6
TOTAL_ROWS = 16


def tiles_kernel(
    pairs_hbm,
    load_ref,
    docs_index_ref,
    vocab_index_ref,
    doc_hbm,
    word_hbm,
    weights_hbm,
    counts_hbm,
    doc_parts_out,
    keep_out,
    send_out,
    doc_next_out,
    pairs_ref,
    weights_ref,
    doc_sums,
    word_sums,
    doc_rows,
    word_rows,
    counts_buf,
    slots,
    item_doc,
    item_of,
    filled,
    topics_sem,
    counts_sem,
    sums_sem,
):
    tile_docs, tile_words = counts_hbm.shape[1:]
    blocks = word_hbm.shape[0] // tile_words
    doc_blocks = doc_hbm.shape[0] // tile_docs
    load = load_ref[0, 0]
    y, own_core = docs_index_ref[0] // (N_X_LO * N_CORE), lax.rem(docs_index_ref[0], N_CORE)
    z = vocab_index_ref[0] // N_X_HI
    dest_blocks = blocks // (N_Y * N_X_LO * N_CORE)

    half_docs = tile_docs // N_X_HI
    half_rows = half_docs + TOTAL_ROWS

    def word_place(block):
        dest = block // dest_blocks
        core = lax.rem(dest, N_CORE)
        x_lo = lax.rem(dest // N_CORE, N_X_LO)
        step = lax.rem(dest // (N_CORE * N_X_LO) - y + N_Y, N_Y)
        other = jnp.where(core == own_core, 0, 1)
        place = jnp.where(step == 0, 3, jnp.where(step == 2, 0, (step + 1) // 2))
        part = (other * N_Y + place) * N_X_LO + x_lo
        return (part * dest_blocks + lax.rem(block, dest_blocks)) * tile_words

    doc_copy = pltpu.make_async_copy(doc_hbm, doc_rows, topics_sem.at[0])
    word_copy = pltpu.make_async_copy(word_hbm, word_rows, topics_sem.at[1])
    pairs_copy = pltpu.make_async_copy(pairs_hbm.at[0], pairs_ref, topics_sem.at[2])
    weights_copy = pltpu.make_async_copy(weights_hbm, weights_ref, topics_sem.at[3])
    pairs_copy.start()
    doc_copy.start()
    word_copy.start()
    weights_copy.start()

    def clear_item(item, carry):
        item_doc[item] = 0
        for n in range(WIDE):
            slots[item * WIDE + n] = -1
        return carry

    lax.fori_loop(0, item_doc.shape[0], clear_item, 0)
    for b in range(doc_blocks):
        filled[b] = 0

    pairs_copy.wait()

    def sort_slot(s, made):
        b = pairs_ref[0, s] // blocks
        taken = filled[b]
        item = jnp.where(taken == 0, made, item_of[b])
        item_of[b] = item
        item_doc[item] = b
        slots[item * WIDE + taken] = s
        filled[b] = lax.rem(taken + 1, WIDE)
        return made + jnp.where(taken == 0, 1, 0)

    made = lax.fori_loop(0, load, sort_slot, 0)
    rounds = (made + AT_ONCE - 1) // AT_ONCE

    def copies(item):
        ring = lax.rem(item, SLOTS)
        return [
            pltpu.make_async_copy(
                counts_hbm.at[jnp.maximum(slots[item * WIDE + n], 0)],
                counts_buf.at[ring, n],
                counts_sem.at[ring, n],
            )
            for n in range(WIDE)
        ]

    def start(n):
        @pl.when(n < rounds)
        def _():
            for item in range(AT_ONCE):
                for copy in copies(n * AT_ONCE + item):
                    copy.start()

    for ahead in range(SLOTS // AT_ONCE - 1):
        start(ahead)

    doc_sums[...] = jnp.zeros_like(doc_sums)
    word_sums[...] = jnp.zeros_like(word_sums)
    doc_copy.wait()
    word_copy.wait()
    weights_copy.wait()

    def load_item(item):
        doc_at = pl.multiple_of(item_doc[item] * tile_docs, tile_docs)
        docs = doc_rows[pl.ds(doc_at, tile_docs), :]
        words, weight, counts, word_blocks = [], [], [], []
        for n in range(WIDE):
            slot = slots[item * WIDE + n]
            block = lax.rem(pairs_ref[0, jnp.maximum(slot, 0)], blocks)
            word_at = pl.multiple_of(block * tile_words, tile_words)
            words.append(word_rows[pl.ds(word_at, tile_words), :])
            weight.append(weights_ref[pl.ds(block, 1), :] * jnp.where(slot >= 0, 1.0, 0.0))
            counts.append(counts_buf[lax.rem(item, SLOTS), n])
            word_blocks.append(block)
        words = jnp.concatenate(words, axis=0)
        weight = jnp.concatenate(weight, axis=1)
        counts = jnp.concatenate(counts, axis=1)
        return docs, words, weight, counts, word_blocks

    def count_ratio(docs, words, weight, counts):
        predicted = lax.dot_general(
            docs, words, (((1,), (1,)), ((), ())), preferred_element_type=jnp.float32
        )
        weighted = (counts.astype(jnp.float32) * weight).astype(jnp.bfloat16)
        return (weighted.astype(jnp.float32) / predicted).astype(jnp.bfloat16)

    def add_terms(item, ratio, docs, words, word_blocks):
        doc_step = lax.rem(item_doc[item] - z + N_Z, N_Z)
        doc_terms = jnp.dot(ratio, words, preferred_element_type=jnp.float32)
        for half in range(N_X_HI):
            to = pl.multiple_of((doc_step * N_X_HI + half) * half_rows, TOTAL_ROWS)
            doc_sums[pl.ds(to, half_docs), :] += doc_terms[half * half_docs : (half + 1) * half_docs]
        terms = lax.dot_general(
            ratio, docs, (((0,), (0,)), ((), ())), preferred_element_type=jnp.float32
        )
        for n, block in enumerate(word_blocks):
            to = pl.multiple_of(word_place(block), tile_words)
            word_sums[pl.ds(to, tile_words), :] += terms[n * tile_words : (n + 1) * tile_words]

    def run_items(n, carry):
        start(n + SLOTS // AT_ONCE - 1)
        items = [n * AT_ONCE + item for item in range(AT_ONCE)]
        for item in items:
            for copy in copies(item):
                copy.wait()
        loaded = [load_item(item) for item in items]
        ratios = [count_ratio(*fields[:4]) for fields in loaded]
        for item, ratio, (docs, words, _, _, word_blocks) in zip(items, ratios, loaded):
            add_terms(item, ratio, docs, words, word_blocks)
        return carry

    lax.fori_loop(0, rounds, run_items, 0)

    def leave(n, source, target):
        copy = pltpu.make_async_copy(source, target, sums_sem.at[n])
        copy.start()
        return copy

    leaving = []
    start_row = N_Y * N_X_LO * dest_blocks * tile_words
    for out in send_out:
        leaving.append(leave(len(leaving), word_sums.at[pl.ds(start_row, out.shape[0])], out))
        start_row += out.shape[0]
    total = jnp.zeros((1, doc_rows.shape[1]), jnp.float32)
    for step in range(N_Z):
        for half in range(N_X_HI):
            at = pl.multiple_of(lax.rem(z + step, N_Z) * tile_docs + half * half_docs, half_docs)
            topics = doc_rows[pl.ds(at, half_docs), :].astype(jnp.float32)
            sums = doc_sums[pl.ds((step * N_X_HI + half) * half_rows, half_docs), :]
            total = total + jnp.sum(topics * sums, axis=0, keepdims=True)
    total = jnp.broadcast_to(total * TOTAL_SCALE, (TOTAL_ROWS, doc_rows.shape[1]))
    for n in range(N_Z * N_X_HI):
        doc_sums[(n + 1) * half_rows - TOTAL_ROWS : (n + 1) * half_rows, :] = total
    for step in range(N_Z):
        source = doc_sums.at[pl.ds(step * N_X_HI * half_rows, N_X_HI * half_rows)]
        leaving.append(leave(len(leaving), source, doc_parts_out[step]))
    start_row = 0
    for out in keep_out:
        leaving.append(leave(len(leaving), word_sums.at[pl.ds(start_row, out.shape[0])], out))
        start_row += out.shape[0]
    for copy in leaving:
        copy.wait()


def in_hbm(value):
    return pltpu.with_memory_space_constraint(value, pltpu.HBM)


def run_tiles(
    pair_list, own_load, docs_index, vocab_index, doc_topics, word_topics, weight_table, counts_all
):
    slots = pair_list.shape[-1]
    tile_docs, tile_words = counts_all.shape[1:]
    topics = doc_topics.shape[1]
    doc_blocks = doc_topics.shape[0] // tile_docs
    items = -(-slots // WIDE) + doc_blocks + AT_ONCE
    doc_rows = doc_topics.shape[0] // N_Z + N_X_HI * TOTAL_ROWS
    doc_part = jax.ShapeDtypeStruct((doc_rows, topics), jnp.float32)
    word_rows = word_topics.shape[0] // (N_CORE * N_Y)
    first_part = jax.ShapeDtypeStruct((word_rows, topics), jnp.float32)
    later_part = jax.ShapeDtypeStruct(((N_Y - 1) * word_rows, topics), jnp.float32)
    smem = pl.BlockSpec(memory_space=pltpu.SMEM)
    source = pl.BlockSpec(memory_space=pltpu.HBM)
    hbm = pl.BlockSpec(memory_space=pl.ANY)
    return pl.pallas_call(
        tiles_kernel,
        out_shape=(
            (doc_part,) * N_Z,
            (first_part, later_part),
            (first_part, later_part),
            jax.ShapeDtypeStruct(doc_topics.shape, jnp.float32),
        ),
        in_specs=[source] + [smem] * 3 + [source] * 4,
        out_specs=((hbm,) * N_Z, (hbm,) * 2, (hbm,) * 2, source),
        scratch_shapes=[
            pltpu.SMEM(pair_list.shape[1:], jnp.int32),
            pltpu.VMEM(weight_table.shape, jnp.float32),
            pltpu.VMEM((N_Z * doc_rows, topics), jnp.float32),
            pltpu.VMEM(word_topics.shape, jnp.float32),
            pltpu.VMEM(doc_topics.shape, doc_topics.dtype),
            pltpu.VMEM(word_topics.shape, word_topics.dtype),
            pltpu.VMEM((SLOTS, WIDE, tile_docs, tile_words), counts_all.dtype),
            pltpu.SMEM((items * WIDE,), jnp.int32),
            pltpu.SMEM((items,), jnp.int32),
            pltpu.SMEM((doc_blocks,), jnp.int32),
            pltpu.SMEM((doc_blocks,), jnp.int32),
            pltpu.SemaphoreType.DMA((4,)),
            pltpu.SemaphoreType.DMA((SLOTS, WIDE)),
            pltpu.SemaphoreType.DMA((N_Z + 4,)),
        ],
        compiler_params=pltpu.CompilerParams(vmem_limit_bytes=48 << 20),
        name="tiles",
    )(
        in_hbm(pair_list),
        own_load,
        docs_index,
        vocab_index,
        in_hbm(doc_topics),
        word_topics,
        in_hbm(weight_table),
        counts_all,
    )


def moves(axis, size, move):
    return lambda value: lax.ppermute(value, axis, [(n, move(n) % size) for n in range(size)])


def to_half(value):
    return value.astype(jnp.float16)


def to_float(value):
    return value.astype(jnp.float32)


def rows_around(value, before, after):
    return lax.pad(value, jnp.zeros((), value.dtype), ((before, after, 0), (0, 0, 0)))


def on_device(doc_topics, word_topics, word_weights, tile_pairs, tile_counts, tile_load):
    n_docs, n_vocab = lax.axis_size("docs"), lax.axis_size("vocab")
    docs_index, vocab_index = lax.axis_index("docs"), lax.axis_index("vocab")
    x_lo = docs_index // N_CORE % N_X_LO
    z, x_hi = vocab_index // N_X_HI, vocab_index % N_X_HI
    to_core = moves("docs", n_docs, lambda n: n ^ 1)
    to_x_lo = moves("docs", n_docs, lambda n: n ^ N_CORE)
    y_up = moves("docs", n_docs, lambda n: n + N_X_LO * N_CORE)
    y_down = moves("docs", n_docs, lambda n: n - N_X_LO * N_CORE)
    y_pair = moves("docs", n_docs, lambda n: n ^ (N_X_LO * N_CORE))
    y_cross = moves("docs", n_docs, lambda n: n ^ ((N_Y - 1) * N_X_LO * N_CORE))
    to_x_hi = moves("vocab", n_vocab, lambda n: n ^ 1)
    z_up = moves("vocab", n_vocab, lambda n: n + N_X_HI)
    z_across = moves("vocab", n_vocab, lambda n: n + 2 * N_X_HI)
    z_down = moves("vocab", n_vocab, lambda n: n - N_X_HI)

    counts_all = tile_counts[0, 0]
    tile_words = counts_all.shape[2]
    blocks = word_topics.shape[0] // tile_words
    weight_table = word_weights.reshape(blocks, tile_words)
    doc_parts, keep, send, doc_next = run_tiles(
        tile_pairs,
        tile_load,
        docs_index.reshape(1),
        vocab_index.reshape(1),
        doc_topics,
        word_topics,
        weight_table,
        counts_all,
    )

    meet = lambda *values: lax.optimization_barrier(values)
    near_rows = keep[0].shape[0]
    word_rows = near_rows // N_X_LO
    doc_rows = doc_parts[0].shape[0] // N_X_HI

    part = [piece * DOC_SCALE for piece in doc_parts]
    word_far = to_core(send[0])
    doc_below, doc_above, doc_across = (
        move(to_half(part[step])) for move, step in ((z_up, 1), (z_down, 3), (z_across, 2))
    )

    far = (keep[0] + word_far) * WORD_SCALE
    word_up = y_up(to_half(far[:word_rows]))
    word_down = y_down(to_half(far[word_rows:]))
    near_far = to_core(send[1])
    word_up, word_down, near_far, doc_below, doc_above, doc_across = meet(
        word_up, word_down, near_far, doc_below, doc_above, doc_across
    )

    above = (keep[1][:near_rows] + near_far[:near_rows]) * WORD_SCALE
    below = (
        keep[1][near_rows : 2 * near_rows] + near_far[near_rows : 2 * near_rows]
    ) * WORD_SCALE
    word_below = y_up(to_half(above + rows_around(to_float(word_up), 0, word_rows)))
    word_above = y_down(to_half(below + rows_around(to_float(word_down), word_rows, 0)))

    def doc_half(which):
        rows = [
            lax.dynamic_slice_in_dim(value, which * doc_rows, doc_rows, 0)
            for value in (doc_parts[0], doc_below, doc_above, doc_across)
        ]
        return rows[0] * DOC_SCALE + to_float(rows[1]) + to_float(rows[2]) + to_float(rows[3])

    doc_mine, doc_other = doc_half(x_hi), doc_half(1 - x_hi)
    doc_sums = (doc_mine + to_float(to_x_hi(to_half(doc_other)))) / DOC_SCALE
    own_rows = doc_topics.shape[0] // n_vocab
    own_docs = lax.dynamic_slice_in_dim(doc_topics, vocab_index * own_rows, own_rows, 0)
    doc_scaled = own_docs.astype(jnp.float32) * doc_sums[:own_rows] + prior_doc
    doc_block = to_half(
        doc_topics.shape[1] * doc_scaled / jnp.sum(doc_scaled, axis=1, keepdims=True)
    )
    doc_far = to_x_hi(doc_block)
    column = doc_sums[own_rows : own_rows + 1] / TOTAL_SCALE
    column = column + to_core(column)
    column = column + to_x_lo(column)
    word_below, word_above, doc_block, doc_far, column = meet(
        word_below, word_above, doc_block, doc_far, column
    )

    def word_half(which):
        at = which * word_rows
        here = lax.dynamic_slice_in_dim(keep[1], 2 * near_rows + at, word_rows, 0)
        far = lax.dynamic_slice_in_dim(near_far, 2 * near_rows + at, word_rows, 0)
        below = lax.dynamic_slice_in_dim(word_below, at, word_rows, 0)
        above = lax.dynamic_slice_in_dim(word_above, at, word_rows, 0)
        return (here + far) * WORD_SCALE + to_float(below) + to_float(above)

    word_far = to_x_lo(to_half(word_half(1 - x_lo)))
    doc_here = rows_around(jnp.where(x_hi == 0, doc_block, doc_far), 0, own_rows) + rows_around(
        jnp.where(x_hi == 0, doc_far, doc_block), own_rows, 0
    )
    doc_below, doc_above, doc_across = z_up(doc_here), z_down(doc_here), z_across(doc_here)
    column = column + y_pair(column)
    column = column + y_cross(column)
    for step, value in ((0, doc_here), (1, doc_above), (3, doc_below), (2, doc_across)):
        at = (z + step) % N_Z * (N_X_HI * own_rows)
        doc_next = lax.dynamic_update_slice_in_dim(doc_next, to_float(value), at, 0)
    row_count = word_topics.shape[0] // n_docs
    word_sums = (word_half(x_lo) + to_float(word_far)) / WORD_SCALE
    vocab_total = word_topics.shape[0] * n_vocab
    own_words = lax.dynamic_slice_in_dim(word_topics, docs_index * row_count, row_count, 0)
    word_scaled = own_words.astype(jnp.float32) * word_sums + prior_word
    word_next = vocab_total * word_scaled / (column + vocab_total * prior_word)
    return (doc_next, word_next)


def solution(mesh):
    placed = (
        P("docs", None),
        P("vocab", None),
        P("vocab"),
        P("docs", "vocab", None),
        P("docs", "vocab", None, None, None),
        P("docs", "vocab"),
    )
    return jax.shard_map(
        on_device,
        mesh=mesh,
        in_specs=placed,
        out_specs=(P("docs", None), P(("vocab", "docs"), None)),
        check_vma=False,
    )
```

```python
import jax
import jax.numpy as jnp
from jax import lax
from jax.experimental import pallas as pl
from jax.experimental.pallas import tpu as pltpu
from jax.sharding import PartitionSpec as P

prior_doc = 0.5
prior_word = 0.01
WIDE = 4
SLOTS = 8
AT_ONCE = 2
N_Y, N_X_LO, N_CORE = 4, 2, 2
N_Z, N_X_HI = 4, 2
WORD_SCALE = 2.0**-7
DOC_SCALE = 2.0**-8
TOTAL_SCALE = 2.0**-6
TOTAL_ROWS = 16


def tiles_kernel(
    pairs_hbm,
    load_ref,
    docs_index_ref,
    vocab_index_ref,
    doc_hbm,
    word_hbm,
    weights_hbm,
    counts_hbm,
    doc_parts_out,
    keep_out,
    send_out,
    doc_next_out,
    pairs_ref,
    weights_ref,
    doc_sums,
    word_sums,
    doc_rows,
    word_rows,
    counts_buf,
    slots,
    item_doc,
    item_of,
    filled,
    topics_sem,
    counts_sem,
    sums_sem,
):
    tile_docs, tile_words = counts_hbm.shape[1:]
    blocks = word_hbm.shape[0] // tile_words
    doc_blocks = doc_hbm.shape[0] // tile_docs
    load = load_ref[0, 0]
    y, own_core = docs_index_ref[0] // (N_X_LO * N_CORE), lax.rem(docs_index_ref[0], N_CORE)
    z = vocab_index_ref[0] // N_X_HI
    dest_blocks = blocks // (N_Y * N_X_LO * N_CORE)

    half_docs = tile_docs // N_X_HI
    half_rows = half_docs + TOTAL_ROWS

    def word_place(block):
        dest = block // dest_blocks
        core = lax.rem(dest, N_CORE)
        x_lo = lax.rem(dest // N_CORE, N_X_LO)
        step = lax.rem(dest // (N_CORE * N_X_LO) - y + N_Y, N_Y)
        other = jnp.where(core == own_core, 0, 1)
        place = jnp.where(step == 0, 3, jnp.where(step == 2, 0, (step + 1) // 2))
        part = (other * N_Y + place) * N_X_LO + x_lo
        return (part * dest_blocks + lax.rem(block, dest_blocks)) * tile_words

    doc_copy = pltpu.make_async_copy(doc_hbm, doc_rows, topics_sem.at[0])
    word_copy = pltpu.make_async_copy(word_hbm, word_rows, topics_sem.at[1])
    pairs_copy = pltpu.make_async_copy(pairs_hbm.at[0], pairs_ref, topics_sem.at[2])
    weights_copy = pltpu.make_async_copy(weights_hbm, weights_ref, topics_sem.at[3])
    pairs_copy.start()
    doc_copy.start()
    word_copy.start()
    weights_copy.start()

    def clear_item(item, carry):
        item_doc[item] = 0
        for n in range(WIDE):
            slots[item * WIDE + n] = -1
        return carry

    lax.fori_loop(0, item_doc.shape[0], clear_item, 0)
    for b in range(doc_blocks):
        filled[b] = 0

    pairs_copy.wait()

    def sort_slot(s, made):
        b = pairs_ref[0, s] // blocks
        taken = filled[b]
        item = jnp.where(taken == 0, made, item_of[b])
        item_of[b] = item
        item_doc[item] = b
        slots[item * WIDE + taken] = s
        filled[b] = lax.rem(taken + 1, WIDE)
        return made + jnp.where(taken == 0, 1, 0)

    made = lax.fori_loop(0, load, sort_slot, 0)
    rounds = (made + AT_ONCE - 1) // AT_ONCE

    def copies(item):
        ring = lax.rem(item, SLOTS)
        return [
            pltpu.make_async_copy(
                counts_hbm.at[jnp.maximum(slots[item * WIDE + n], 0)],
                counts_buf.at[ring, n],
                counts_sem.at[ring, n],
            )
            for n in range(WIDE)
        ]

    def start(n):
        @pl.when(n < rounds)
        def _():
            for item in range(AT_ONCE):
                for copy in copies(n * AT_ONCE + item):
                    copy.start()

    for ahead in range(SLOTS // AT_ONCE - 1):
        start(ahead)

    doc_sums[...] = jnp.zeros_like(doc_sums)
    word_sums[...] = jnp.zeros_like(word_sums)
    doc_copy.wait()
    word_copy.wait()
    weights_copy.wait()

    def load_item(item):
        doc_at = pl.multiple_of(item_doc[item] * tile_docs, tile_docs)
        docs = doc_rows[pl.ds(doc_at, tile_docs), :]
        words, weight, counts, word_blocks = [], [], [], []
        for n in range(WIDE):
            slot = slots[item * WIDE + n]
            block = lax.rem(pairs_ref[0, jnp.maximum(slot, 0)], blocks)
            word_at = pl.multiple_of(block * tile_words, tile_words)
            words.append(word_rows[pl.ds(word_at, tile_words), :])
            weight.append(weights_ref[pl.ds(block, 1), :] * jnp.where(slot >= 0, 1.0, 0.0))
            counts.append(counts_buf[lax.rem(item, SLOTS), n])
            word_blocks.append(block)
        words = jnp.concatenate(words, axis=0)
        weight = jnp.concatenate(weight, axis=1)
        counts = jnp.concatenate(counts, axis=1)
        return docs, words, weight, counts, word_blocks

    def count_ratio(docs, words, weight, counts):
        predicted = lax.dot_general(
            docs, words, (((1,), (1,)), ((), ())), preferred_element_type=jnp.float32
        )
        weighted = (counts.astype(jnp.float32) * weight).astype(jnp.bfloat16)
        return (weighted.astype(jnp.float32) / predicted).astype(jnp.bfloat16)

    def add_terms(item, ratio, docs, words, word_blocks):
        doc_step = lax.rem(item_doc[item] - z + N_Z, N_Z)
        doc_terms = jnp.dot(ratio, words, preferred_element_type=jnp.float32)
        for half in range(N_X_HI):
            to = pl.multiple_of((doc_step * N_X_HI + half) * half_rows, TOTAL_ROWS)
            doc_sums[pl.ds(to, half_docs), :] += doc_terms[half * half_docs : (half + 1) * half_docs]
        terms = lax.dot_general(
            ratio, docs, (((0,), (0,)), ((), ())), preferred_element_type=jnp.float32
        )
        for n, block in enumerate(word_blocks):
            to = pl.multiple_of(word_place(block), tile_words)
            word_sums[pl.ds(to, tile_words), :] += terms[n * tile_words : (n + 1) * tile_words]

    def run_items(n, carry):
        start(n + SLOTS // AT_ONCE - 1)
        items = [n * AT_ONCE + item for item in range(AT_ONCE)]
        for item in items:
            for copy in copies(item):
                copy.wait()
        loaded = [load_item(item) for item in items]
        ratios = [count_ratio(*fields[:4]) for fields in loaded]
        for item, ratio, (docs, words, _, _, word_blocks) in zip(items, ratios, loaded):
            add_terms(item, ratio, docs, words, word_blocks)
        return carry

    lax.fori_loop(0, rounds, run_items, 0)

    def leave(n, source, target):
        copy = pltpu.make_async_copy(source, target, sums_sem.at[n])
        copy.start()
        return copy

    leaving = []
    start_row = N_Y * N_X_LO * dest_blocks * tile_words
    for out in send_out:
        leaving.append(leave(len(leaving), word_sums.at[pl.ds(start_row, out.shape[0])], out))
        start_row += out.shape[0]
    total = jnp.zeros((1, doc_rows.shape[1]), jnp.float32)
    for step in range(N_Z):
        for half in range(N_X_HI):
            at = pl.multiple_of(lax.rem(z + step, N_Z) * tile_docs + half * half_docs, half_docs)
            topics = doc_rows[pl.ds(at, half_docs), :].astype(jnp.float32)
            sums = doc_sums[pl.ds((step * N_X_HI + half) * half_rows, half_docs), :]
            total = total + jnp.sum(topics * sums, axis=0, keepdims=True)
    total = jnp.broadcast_to(total * TOTAL_SCALE, (TOTAL_ROWS, doc_rows.shape[1]))
    for n in range(N_Z * N_X_HI):
        doc_sums[(n + 1) * half_rows - TOTAL_ROWS : (n + 1) * half_rows, :] = total
    for step in range(N_Z):
        source = doc_sums.at[pl.ds(step * N_X_HI * half_rows, N_X_HI * half_rows)]
        leaving.append(leave(len(leaving), source, doc_parts_out[step]))
    start_row = 0
    for out in keep_out:
        leaving.append(leave(len(leaving), word_sums.at[pl.ds(start_row, out.shape[0])], out))
        start_row += out.shape[0]
    for copy in leaving:
        copy.wait()


def in_hbm(value):
    return pltpu.with_memory_space_constraint(value, pltpu.HBM)


def run_tiles(
    pair_list, own_load, docs_index, vocab_index, doc_topics, word_topics, weight_table, counts_all
):
    slots = pair_list.shape[-1]
    tile_docs, tile_words = counts_all.shape[1:]
    topics = doc_topics.shape[1]
    doc_blocks = doc_topics.shape[0] // tile_docs
    items = -(-slots // WIDE) + doc_blocks + AT_ONCE
    doc_rows = doc_topics.shape[0] // N_Z + N_X_HI * TOTAL_ROWS
    doc_part = jax.ShapeDtypeStruct((doc_rows, topics), jnp.float32)
    word_rows = word_topics.shape[0] // (N_CORE * N_Y)
    first_part = jax.ShapeDtypeStruct((word_rows, topics), jnp.float32)
    later_part = jax.ShapeDtypeStruct(((N_Y - 1) * word_rows, topics), jnp.float32)
    smem = pl.BlockSpec(memory_space=pltpu.SMEM)
    source = pl.BlockSpec(memory_space=pltpu.HBM)
    hbm = pl.BlockSpec(memory_space=pl.ANY)
    return pl.pallas_call(
        tiles_kernel,
        out_shape=(
            (doc_part,) * N_Z,
            (first_part, later_part),
            (first_part, later_part),
            jax.ShapeDtypeStruct(doc_topics.shape, jnp.float32),
        ),
        in_specs=[source] + [smem] * 3 + [source] * 4,
        out_specs=((hbm,) * N_Z, (hbm,) * 2, (hbm,) * 2, source),
        scratch_shapes=[
            pltpu.SMEM(pair_list.shape[1:], jnp.int32),
            pltpu.VMEM(weight_table.shape, jnp.float32),
            pltpu.VMEM((N_Z * doc_rows, topics), jnp.float32),
            pltpu.VMEM(word_topics.shape, jnp.float32),
            pltpu.VMEM(doc_topics.shape, doc_topics.dtype),
            pltpu.VMEM(word_topics.shape, word_topics.dtype),
            pltpu.VMEM((SLOTS, WIDE, tile_docs, tile_words), counts_all.dtype),
            pltpu.SMEM((items * WIDE,), jnp.int32),
            pltpu.SMEM((items,), jnp.int32),
            pltpu.SMEM((doc_blocks,), jnp.int32),
            pltpu.SMEM((doc_blocks,), jnp.int32),
            pltpu.SemaphoreType.DMA((4,)),
            pltpu.SemaphoreType.DMA((SLOTS, WIDE)),
            pltpu.SemaphoreType.DMA((N_Z + 4,)),
        ],
        compiler_params=pltpu.CompilerParams(vmem_limit_bytes=48 << 20),
        name="tiles",
    )(
        in_hbm(pair_list),
        own_load,
        docs_index,
        vocab_index,
        in_hbm(doc_topics),
        word_topics,
        in_hbm(weight_table),
        counts_all,
    )


def moves(axis, size, move):
    return lambda value: lax.ppermute(value, axis, [(n, move(n) % size) for n in range(size)])


def to_half(value):
    return value.astype(jnp.float16)


def to_float(value):
    return value.astype(jnp.float32)


def rows_around(value, before, after):
    return lax.pad(value, jnp.zeros((), value.dtype), ((before, after, 0), (0, 0, 0)))


def on_device(doc_topics, word_topics, word_weights, tile_pairs, tile_counts, tile_load):
    n_docs, n_vocab = lax.axis_size("docs"), lax.axis_size("vocab")
    docs_index, vocab_index = lax.axis_index("docs"), lax.axis_index("vocab")
    x_lo = docs_index // N_CORE % N_X_LO
    z, x_hi = vocab_index // N_X_HI, vocab_index % N_X_HI
    to_core = moves("docs", n_docs, lambda n: n ^ 1)
    to_x_lo = moves("docs", n_docs, lambda n: n ^ N_CORE)
    y_up = moves("docs", n_docs, lambda n: n + N_X_LO * N_CORE)
    y_down = moves("docs", n_docs, lambda n: n - N_X_LO * N_CORE)
    y_pair = moves("docs", n_docs, lambda n: n ^ (N_X_LO * N_CORE))
    y_cross = moves("docs", n_docs, lambda n: n ^ ((N_Y - 1) * N_X_LO * N_CORE))
    to_x_hi = moves("vocab", n_vocab, lambda n: n ^ 1)
    z_up = moves("vocab", n_vocab, lambda n: n + N_X_HI)
    z_across = moves("vocab", n_vocab, lambda n: n + 2 * N_X_HI)
    z_down = moves("vocab", n_vocab, lambda n: n - N_X_HI)

    counts_all = tile_counts[0, 0]
    tile_words = counts_all.shape[2]
    blocks = word_topics.shape[0] // tile_words
    weight_table = word_weights.reshape(blocks, tile_words)
    doc_parts, keep, send, doc_next = run_tiles(
        tile_pairs,
        tile_load,
        docs_index.reshape(1),
        vocab_index.reshape(1),
        doc_topics,
        word_topics,
        weight_table,
        counts_all,
    )

    meet = lambda *values: lax.optimization_barrier(values)
    near_rows = keep[0].shape[0]
    word_rows = near_rows // N_X_LO
    doc_rows = doc_parts[0].shape[0] // N_X_HI

    part = [piece * DOC_SCALE for piece in doc_parts]
    word_far = to_core(send[0])
    doc_below, doc_above, doc_across = (
        move(to_half(part[step])) for move, step in ((z_up, 1), (z_down, 3), (z_across, 2))
    )

    far = (keep[0] + word_far) * WORD_SCALE
    word_up = y_up(to_half(far[:word_rows]))
    word_down = y_down(to_half(far[word_rows:]))
    near_far = to_core(send[1])
    word_up, word_down, near_far, doc_below, doc_above, doc_across = meet(
        word_up, word_down, near_far, doc_below, doc_above, doc_across
    )

    above = (keep[1][:near_rows] + near_far[:near_rows]) * WORD_SCALE
    below = (
        keep[1][near_rows : 2 * near_rows] + near_far[near_rows : 2 * near_rows]
    ) * WORD_SCALE
    word_below = y_up(to_half(above + rows_around(to_float(word_up), 0, word_rows)))
    word_above = y_down(to_half(below + rows_around(to_float(word_down), word_rows, 0)))

    def doc_half(which):
        rows = [
            lax.dynamic_slice_in_dim(value, which * doc_rows, doc_rows, 0)
            for value in (doc_parts[0], doc_below, doc_above, doc_across)
        ]
        return rows[0] * DOC_SCALE + to_float(rows[1]) + to_float(rows[2]) + to_float(rows[3])

    doc_mine, doc_other = doc_half(x_hi), doc_half(1 - x_hi)
    doc_sums = (doc_mine + to_float(to_x_hi(to_half(doc_other)))) / DOC_SCALE
    own_rows = doc_topics.shape[0] // n_vocab
    own_docs = lax.dynamic_slice_in_dim(doc_topics, vocab_index * own_rows, own_rows, 0)
    doc_scaled = own_docs.astype(jnp.float32) * doc_sums[:own_rows] + prior_doc
    doc_block = to_half(
        doc_topics.shape[1] * doc_scaled / jnp.sum(doc_scaled, axis=1, keepdims=True)
    )
    doc_far = to_x_hi(doc_block)
    column = doc_sums[own_rows : own_rows + 1] / TOTAL_SCALE
    column = column + to_core(column)
    column = column + to_x_lo(column)
    word_below, word_above, doc_block, doc_far, column = meet(
        word_below, word_above, doc_block, doc_far, column
    )

    def word_half(which):
        at = which * word_rows
        here = lax.dynamic_slice_in_dim(keep[1], 2 * near_rows + at, word_rows, 0)
        far = lax.dynamic_slice_in_dim(near_far, 2 * near_rows + at, word_rows, 0)
        below = lax.dynamic_slice_in_dim(word_below, at, word_rows, 0)
        above = lax.dynamic_slice_in_dim(word_above, at, word_rows, 0)
        return (here + far) * WORD_SCALE + to_float(below) + to_float(above)

    word_mine, word_far = meet(word_half(x_lo), to_half(word_half(1 - x_lo)))
    word_far = to_x_lo(word_far)
    doc_here = rows_around(jnp.where(x_hi == 0, doc_block, doc_far), 0, own_rows) + rows_around(
        jnp.where(x_hi == 0, doc_far, doc_block), own_rows, 0
    )
    doc_below, doc_above, doc_across = z_up(doc_here), z_down(doc_here), z_across(doc_here)
    column = column + y_pair(column)
    column = column + y_cross(column)
    for step, value in ((0, doc_here), (1, doc_above), (3, doc_below), (2, doc_across)):
        at = (z + step) % N_Z * (N_X_HI * own_rows)
        doc_next = lax.dynamic_update_slice_in_dim(doc_next, to_float(value), at, 0)
    row_count = word_topics.shape[0] // n_docs
    word_sums = (word_mine + to_float(word_far)) / WORD_SCALE
    vocab_total = word_topics.shape[0] * n_vocab
    own_words = lax.dynamic_slice_in_dim(word_topics, docs_index * row_count, row_count, 0)
    word_scaled = own_words.astype(jnp.float32) * word_sums + prior_word
    word_next = vocab_total * word_scaled / (column + vocab_total * prior_word)
    return (doc_next, word_next)


def solution(mesh):
    placed = (
        P("docs", None),
        P("vocab", None),
        P("vocab"),
        P("docs", "vocab", None),
        P("docs", "vocab", None, None, None),
        P("docs", "vocab"),
    )
    return jax.shard_map(
        on_device,
        mesh=mesh,
        in_specs=placed,
        out_specs=(P("docs", None), P(("vocab", "docs"), None)),
        check_vma=False,
    )
```
